32 devices in a mesh: dp: 16 (over z, y, x), tensor: 2 (over core).
Axes of the slice: x: 2, y: 2, z: 4, core: 2. Of those that a mesh axis runs over, the one named last changes fastest.
Arguments:
- tokens: bfloat16 [16384, 1024], P(('dp', 'tensor')), may hold values from -6 to 6
- w_query: bfloat16 [1024, 1024], P('dp', 'tensor'), may hold values from -0.1875 to 0.1875
- w_key: bfloat16 [1024, 1024], P('dp', 'tensor'), may hold values from -0.1875 to 0.1875
- w_value: bfloat16 [1024, 1024], P('dp', 'tensor'), may hold values from -0.1875 to 0.1875
- w_gate: bfloat16 [1024, 1024], P('dp', 'tensor'), may hold values from -0.1875 to 0.1875
- w_out: bfloat16 [1024, 1024], P('tensor', 'dp'), may hold values from -0.1875 to 0.1875
- w_first: bfloat16 [1024, 2816], P('dp', 'tensor'), may hold values from -0.1875 to 0.1875
- w_second: bfloat16 [1024, 2816], P('dp', 'tensor'), may hold values from -0.1875 to 0.1875
- w_down: bfloat16 [2816, 1024], P('tensor', 'dp'), may hold values from -0.109375 to 0.109375
- decay_rates: float32 [8], P('tensor'), may hold values from 0.00048828125 to 0.05
- cotangent: bfloat16 [16384, 1024], P(('dp', 'tensor')), may hold values from -6 to 6
Outputs:
- layer_out: bfloat16 [16384, 1024], P(('dp', 'tensor'))
- tokens_grad: float32 [16384, 1024], P(('dp', 'tensor'))
- grad_query: float32 [1024, 1024], P('dp', 'tensor')
- grad_key: float32 [1024, 1024], P('dp', 'tensor')
- grad_value: float32 [1024, 1024], P('dp', 'tensor')
- grad_gate: float32 [1024, 1024], P('dp', 'tensor')
- grad_out: float32 [1024, 1024], P('tensor', 'dp')
- grad_first: float32 [1024, 2816], P('dp', 'tensor')
- grad_second: float32 [1024, 2816], P('dp', 'tensor')
- grad_down: float32 [2816, 1024], P('tensor', 'dp')
The draws below stay inside these ranges and needn't reach their ends.
All inputs are finite; a program needn't handle non-finite values.
Results may differ from the reference program's by a relative error of at most 0.014.
Values may be sent and summed in bfloat16 or wider, within the bound.
No kernel may reach another device: no remote copies, remote signals or barrier semaphores. Data moves between devices by JAX's collectives and lax.ppermute only.
A program may use at most 192 MiB of HBM per device.

```python
import math
import jax
import jax.numpy as jnp
from jax import lax

D = 1024
H = 8
FF = 2816
SEQ = 1024
TOKENS = 16384


def block_levels(own_key, shape, shards, smallest, largest):
    def one(dim, parts):
        heights = jax.random.uniform(jax.random.fold_in(jax.random.fold_in(own_key, 6), dim), (parts,), jnp.float32, smallest / len(shards), largest / len(shards))
        return jnp.repeat(jnp.exp(heights), shape[dim] // parts).reshape((-1,) + (1,) * (len(shape) - dim - 1))

    gain = one(*shards[0])
    for cut in shards[1:]:
        gain = gain * one(*cut)
    return gain


def normal_values(own_key, dims, spread, bound, shards=(), dtype=jnp.bfloat16):
    entries = jax.random.normal(own_key, dims, jnp.float32) * spread
    if len(shards) > 0:
        entries = block_levels(own_key, dims, shards, -0.22, 0.18) * entries
    return jnp.clip(entries, min=-bound, max=bound).astype(dtype)


def setup_inputs(seed: int = 0) -> dict:
    key_of = jax.random.split(jax.random.key(seed), 12)
    return {
        "tokens": normal_values(key_of[0], (TOKENS, D), 1.0, 6.0, ((0, 32),)),
        "w_query": normal_values(key_of[1], (D, D), D ** -0.5, 0.1875, ((0, 16), (1, 2))),
        "w_key": normal_values(key_of[2], (D, D), D ** -0.5, 0.1875, ((0, 16), (1, 2))),
        "w_value": normal_values(key_of[3], (D, D), D ** -0.5, 0.1875, ((0, 16), (1, 2))),
        "w_gate": normal_values(key_of[4], (D, D), D ** -0.5, 0.1875, ((0, 16), (1, 2))),
        "w_out": normal_values(key_of[5], (D, D), D ** -0.5, 0.1875, ((0, 2), (1, 16))),
        "w_first": normal_values(key_of[6], (D, FF), D ** -0.5, 0.1875, ((0, 16), (1, 2))),
        "w_second": normal_values(key_of[7], (D, FF), D ** -0.5, 0.1875, ((0, 16), (1, 2))),
        "w_down": normal_values(key_of[8], (FF, D), FF ** -0.5, 0.109375, ((0, 2), (1, 16))),
        "decay_rates": jnp.clip(jnp.exp(math.log(0.05) - 4.6288867 * jax.random.uniform(key_of[9], (H,), jnp.float32) ** block_levels(key_of[9], (H,), ((0, 2),), -0.2, 0.2)), 0.00048828125, 0.05),
        "cotangent": normal_values(key_of[10], (TOKENS, D), 1.0, 6.0, ((0, 32),)),
    }


eps = 1e-06
precise = lax.Precision.HIGHEST

@jax.custom_vjp
def low(v):
    return lax.optimization_barrier(v.astype(jnp.bfloat16)).astype(jnp.float32)

@jax.custom_vjp
def low_back(v):
    return v

def low_keep(v):
    return (low(v), None)

def low_pass(kept, grad):
    return (grad,)

def back_keep(v):
    return (v, None)

def back_low(kept, grad):
    return (low(grad),)
low.defvjp(low_keep, low_pass)
low_back.defvjp(back_keep, back_low)

def product(left, right):
    return jnp.dot(left, right, precision=precise)

def srms(values):
    return values * lax.rsqrt(lax.optimization_barrier(jnp.mean(values * values, axis=-1, keepdims=True)) + eps)

def decay_tables(rates, size):
    position = jnp.arange(size).astype(jnp.float32)
    distance = position[:, None] - position[None, :]
    causal = distance >= 0
    safe = jnp.where(causal, distance, 0.0)
    inner = jnp.where(causal[None], jnp.exp(-rates[:, None, None] * safe[None]), 0.0)
    ahead = jnp.exp(-rates[None, :] * position[:, None])
    outof = jnp.exp(-rates[None, :] * (size - position[:, None]))
    whole = jnp.exp(-rates * size)
    return (inner, ahead, outof, whole)

def lightning(query, keys, values, rates):
    length, heads, head_size = query.shape
    block = min(512, SEQ // 2)
    blocks = length // block
    inner, ahead, outof, whole = decay_tables(rates, block)

    def advance(state, pieces):
        q_blk, k_blk, v_blk = pieces
        scores = low_back(jnp.einsum('ihd,jhd->hij', q_blk, k_blk, precision=precise))
        weights = low(scores * inner)
        local = jnp.einsum('hij,jhd->ihd', weights, v_blk, precision=precise)
        carried = low_back(jnp.einsum('ihd,hde->ihe', q_blk, low(state), precision=precise)) * ahead[:, :, None]
        k_weighted = low(k_blk * outof[:, :, None])
        increment = low_back(jnp.einsum('jhd,jhe->hde', k_weighted, v_blk, precision=precise))
        state = state * whole[:, None, None] + increment
        return (state, local + carried)

    def split(array):
        return array.reshape(blocks, block, heads, head_size)
    start_state = jnp.zeros((heads, head_size, head_size), jnp.float32)
    _, result = lax.scan(jax.checkpoint(advance), start_state, (split(query), split(keys), split(values)))
    return result.reshape(length, heads * head_size)

def layer(inputs, mats, rates):
    w_query, w_key, w_value, w_gate, w_out, w_first, w_second, w_down = mats
    length = inputs.shape[0]
    heads = rates.shape[0]
    normed_in = low(srms(inputs))
    proj_q = low_back(product(normed_in, w_query))
    proj_k = low_back(product(normed_in, w_key))
    proj_v = low_back(product(normed_in, w_value))
    proj_u = low_back(product(normed_in, w_gate))
    query = low(jax.nn.silu(proj_q)).reshape(length, heads, -1)
    keys = low(jax.nn.silu(proj_k)).reshape(length, heads, -1)
    values = low(proj_v).reshape(length, heads, -1)
    attended = low_back(lightning(query, keys, values, rates))
    gated = low(srms(attended) * proj_u)
    middle = inputs + low_back(product(gated, w_out))
    normed_mid = low(srms(middle))
    first = low_back(product(normed_mid, w_first))
    second = low_back(product(normed_mid, w_second))
    squashed = low(first * second)
    return middle + low_back(product(squashed, w_down))

def reference(tokens, w_query, w_key, w_value, w_gate, w_out, w_first, w_second, w_down, decay_rates, cotangent):
    count_seqs = tokens.shape[0] // SEQ
    inputs = tokens.astype(jnp.float32).reshape(count_seqs, SEQ, D)
    mats = tuple((matrix.astype(jnp.float32) for matrix in (w_query, w_key, w_value, w_gate, w_out, w_first, w_second, w_down)))
    rates = decay_rates.astype(jnp.float32)

    def forward(stacked, *weights):

        def single(sequence):
            return layer(sequence, weights, rates)
        return lax.map(jax.checkpoint(single), stacked)
    outputs, pull = jax.vjp(forward, inputs, *mats)
    grads = pull(cotangent.astype(jnp.float32).reshape(count_seqs, SEQ, D))
    return (outputs.reshape(-1, D).astype(jnp.bfloat16), grads[0].reshape(-1, D), grads[1], grads[2], grads[3], grads[4], grads[5], grads[6], grads[7], grads[8])
```

```python
import functools

import jax
import jax.numpy as jnp
import numpy as np
from jax import lax
from jax.experimental import pallas as pl
from jax.experimental.pallas import tpu as pltpu
from jax.sharding import PartitionSpec as P

eps = 1e-06
wide = jnp.float32
narrow = jnp.bfloat16
window = 5


def dot(left, right, dims):
    return lax.dot_general(left, right, (dims, ((), ())), preferred_element_type=wide)


def nn(left, right):
    return dot(left, right, ((1,), (0,)))


def nt(left, right):
    return dot(left, right, ((1,), (1,)))


def tn(left, right):
    return dot(left, right, ((0,), (0,)))


def inverse_rms(values):
    return lax.rsqrt(jnp.mean(values * values, axis=-1, keepdims=True) + eps)


def norm_back(grad, normed, scale):
    return scale * (grad - normed * jnp.mean(grad * normed, axis=-1, keepdims=True))


def silu_slope(values):
    sigma = jax.nn.sigmoid(values)
    return sigma * (1.0 + values * (1.0 - sigma))


class Exchange:

    def __init__(self, size):
        self.size = size
        self.sent = []

    def __call__(self, array, bit):
        if len(self.sent) >= window:
            array = lax.optimization_barrier((array, self.sent[-window]))[0]
        pairs = [(i, i ^ bit) for i in range(self.size)]
        result = lax.ppermute(array, "dp", pairs)
        self.sent.append(result)
        return result


def inner_bits(size):
    bits = []
    bit = size // 2
    while bit >= 4:
        bits.append(bit)
        bit //= 2
    return bits


def block_offsets(size):
    order = [0]
    for bit in inner_bits(size) + [1, 2]:
        order = order + [entry ^ bit for entry in order]
    return np.array(order, np.int32)


def gather_all(send, shards):
    bits = inner_bits(send.size)
    depth = len(bits)
    count = len(shards)
    held = list(shards)
    pieces = [None] * count
    for step in range(count + depth + 1):
        c = step - depth - 1
        if 0 <= c < count:
            first, side, up = pieces[c]
            if c % 2 == 0:
                pieces[c] = (first, side, up, send(side, 2))
            else:
                pieces[c] = (first, side, up, send(up, 1))
        c = step - depth
        if 0 <= c < count:
            pieces[c] = (held[c], send(held[c], 1), send(held[c], 2))
        for level in range(depth - 1, -1, -1):
            c = step - level
            if 0 <= c < count:
                held[c] = jnp.concatenate([held[c], send(held[c], bits[level])], axis=0)
    return pieces


def scatter(send, grads, turn):
    first, side, up, far = (piece.astype(wide) for piece in grads)
    low = lambda value: value.astype(narrow)
    if turn:
        from_up = send(low(up), 2)
        side = side + send(low(far), 2).astype(wide)
        from_side = send(low(side), 1)
    else:
        from_side = send(low(side), 1)
        up = up + send(low(far), 1).astype(wide)
        from_up = send(low(up), 2)
    total = first + from_side.astype(wide) + from_up.astype(wide)
    for bit in reversed(inner_bits(send.size)):
        half = total.shape[0] // 2
        total = total[:half] + send(low(total[half:]), bit).astype(wide)
    return total


def tables(rate, size):
    row = lax.broadcasted_iota(jnp.int32, (size, 1), 0).astype(wide)
    col = lax.broadcasted_iota(jnp.int32, (1, size), 1).astype(wide)
    ahead = jnp.exp(-rate * row)
    inner = jnp.where(col <= row, ahead * jnp.exp(rate * col), 0.0)
    outof = jnp.exp(-rate * (size - row))
    return inner, ahead, outof


def attend_kernel(turn_ref, rate_ref, q_ref, k_ref, v_ref, o_ref):
    size = q_ref.shape[0] // 2
    inner, ahead, outof = tables(rate_ref[pl.program_id(0)], size)
    turn = turn_ref[0]
    early = pl.ds(pl.multiple_of(turn * size, size), size)
    late = pl.ds(pl.multiple_of((1 - turn) * size, size), size)

    def local(rows):
        weights = (nt(q_ref[rows, :], k_ref[rows, :]) * inner).astype(narrow)
        return nn(weights, v_ref[rows, :])

    weighted = (k_ref[early, :].astype(wide) * outof).astype(narrow)
    state = tn(weighted, v_ref[early, :]).astype(narrow)
    o_ref[early, :] = local(early)
    o_ref[late, :] = local(late) + nn(q_ref[late, :], state) * ahead


def attend_back_kernel(
    turn_ref, rate_ref, q_ref, k_ref, v_ref, g_ref, pq_ref, pk_ref, dq_ref, dk_ref, dv_ref
):
    size = q_ref.shape[0] // 2
    inner, ahead, outof = tables(rate_ref[pl.program_id(0)], size)
    turn = turn_ref[0]
    early = pl.ds(pl.multiple_of(turn * size, size), size)
    late = pl.ds(pl.multiple_of((1 - turn) * size, size), size)

    def local(rows):
        q, k, v, g = (ref[rows, :] for ref in (q_ref, k_ref, v_ref, g_ref))
        weights = (nt(q, k) * inner).astype(narrow)
        grad_scores = (nt(g, v) * inner).astype(narrow)
        return nn(grad_scores, k), tn(grad_scores, q), tn(weights, g)

    def store(rows, dq, dk, dv):
        dq_ref[rows, :] = (dq * silu_slope(pq_ref[rows, :])).astype(narrow)
        dk_ref[rows, :] = (dk * silu_slope(pk_ref[rows, :])).astype(narrow)
        dv_ref[rows, :] = dv.astype(narrow)

    weighted = (k_ref[early, :].astype(wide) * outof).astype(narrow)
    state = tn(weighted, v_ref[early, :]).astype(narrow)
    g_ahead = (g_ref[late, :].astype(wide) * ahead).astype(narrow)
    grad_state = tn(q_ref[late, :], g_ahead).astype(narrow)
    dq, dk, dv = local(late)
    store(late, dq + nt(g_ahead, state), dk, dv)
    dq, dk, dv = local(early)
    store(
        early,
        dq,
        dk + nt(v_ref[early, :], grad_state) * outof,
        dv + nn(weighted, grad_state),
    )


def per_head(kernel, turn, rates, arrays, out_types):
    heads = rates.shape[0]
    length, columns = arrays[0].shape
    spec = pl.BlockSpec((length, columns // heads), lambda h: (0, h))
    scalar = pl.BlockSpec(memory_space=pltpu.SMEM)
    return pl.pallas_call(
        kernel,
        grid=(heads,),
        in_specs=[scalar, scalar] + [spec] * len(arrays),
        out_specs=[spec] * len(out_types),
        out_shape=[jax.ShapeDtypeStruct((length, columns), t) for t in out_types],
    )(turn, rates, *arrays)


def ffn_kernel(*refs, chained):
    n_ref, g_ref, nt_ref, gt_ref, w0, w1, w2, w3 = refs[:8]
    if chained:
        y_in, d_in, y_ref, d_ref, o_ref, s_ref, da_ref, db_ref = refs[8:]
    else:
        y_ref, d_ref, o_ref, s_ref, da_ref, db_ref = refs[8:]
    step = pl.program_id(0)
    tile = y_ref.shape[0]
    n = s_ref.shape[1]
    quarter = w0.shape[0]
    pieces = (w0, w1, w2, w3)
    tiles = n_ref.shape[0] // tile

    @pl.when(step < tiles)
    def _():
        rows = pl.ds(pl.multiple_of(step * tile, tile), tile)
        ab = jnp.zeros((tile, 2 * n), wide)
        ds = jnp.zeros((tile, n), wide)
        for i, ref in enumerate(pieces):
            cols = slice(i * quarter, (i + 1) * quarter)
            ab += nn(n_ref[rows, cols], ref[:, : 2 * n])
            ds += nn(g_ref[rows, cols], ref[:, 2 * n :])
        a = ab[:, :n]
        b = ab[:, n:]
        s = (a * b).astype(narrow)
        da = (ds * b).astype(narrow)
        db = (ds * a).astype(narrow)
        s_ref[rows, :] = s
        da_ref[rows, :] = da
        db_ref[rows, :] = db
        for i, ref in enumerate(pieces):
            cols = slice(i * quarter, (i + 1) * quarter)
            y = nt(s, ref[:, 2 * n :])
            d = nt(da, ref[:, :n]) + nt(db, ref[:, n : 2 * n])
            if chained:
                y = y + y_in[:, cols]
                d = d + d_in[:, cols]
            y_ref[:, cols] = y
            d_ref[:, cols] = d

    @pl.when(step >= tiles)
    def _():
        o_ref[:, :n] = nn(nt_ref[...], da_ref[...]).astype(o_ref.dtype)
        o_ref[:, n : 2 * n] = nn(nt_ref[...], db_ref[...]).astype(o_ref.dtype)
        o_ref[:, 2 * n :] = nn(gt_ref[...], s_ref[...]).astype(o_ref.dtype)


def ffn_chunk(normed, grad, normed_t, grad_t, pieces, sums):
    length, width = normed.shape
    quarter, n3 = pieces[0].shape
    n = n3 // 3
    tile = 256
    tiles = length // tile
    whole = lambda shape: pl.BlockSpec(shape, lambda i: (0, 0))
    rows = pl.BlockSpec((tile, width), lambda i: (jnp.minimum(i, tiles - 1), 0))
    part = pl.BlockSpec((quarter, length), lambda i: (jnp.maximum(i - tiles, 0), 0))
    out_part = pl.BlockSpec((quarter, n3), lambda i: (jnp.maximum(i - tiles, 0), 0))
    chained = sums is not None
    return pl.pallas_call(
        functools.partial(ffn_kernel, chained=chained),
        grid=(tiles + 4,),
        in_specs=[whole((length, width))] * 2
        + [part] * 2
        + [whole((quarter, n3))] * 4
        + ([rows] * 2 if chained else []),
        out_specs=[rows, rows, out_part],
        out_shape=[
            jax.ShapeDtypeStruct((length, width), wide),
            jax.ShapeDtypeStruct((length, width), wide),
            jax.ShapeDtypeStruct((width, n3), narrow),
        ],
        scratch_shapes=[pltpu.VMEM((length, n), narrow)] * 3,
    )(normed, grad, normed_t, grad_t, *pieces, *(sums if chained else ()))


def quarters(array):
    q = array.shape[0] // 4
    return [array[i * q : (i + 1) * q] for i in range(4)]


def ffn_cuts(total):
    cuts = []
    left = total
    while left > 0:
        take = min(512, left)
        cuts.append((total - left, take))
        left -= take
    return cuts


def shards(
    size,
    tokens,
    w_query,
    w_key,
    w_value,
    w_gate,
    w_out,
    w_first,
    w_second,
    w_down,
    decay_rates,
    cotangent,
):
    send = Exchange(size)
    swap = lambda value: lax.ppermute(value, "tensor", [(0, 1), (1, 0)])
    me = lax.axis_index("dp")
    turn = lax.axis_index("tensor").astype(jnp.int32).reshape(1)
    rows, width = tokens.shape
    span = width // size
    offsets = jnp.asarray(np.repeat(block_offsets(size), span))
    place = jnp.bitwise_xor(offsets, me) * span + jnp.arange(width) % span
    shuffle = (jnp.arange(width)[:, None] == place[None, :]).astype(narrow)

    cuts = ffn_cuts(w_first.shape[1])
    down_t = w_down.T
    ffn_shards = [
        jnp.concatenate([w[:, at : at + n] for w in (w_first, w_second, down_t)], axis=1)
        for at, n in cuts
    ]
    gathered = gather_all(send, [w_query, w_key, w_value, w_gate, w_out.T] + ffn_shards)
    full_q, full_k, full_v, full_u, full_o = (
        jnp.concatenate(pieces, axis=0) for pieces in gathered[:5]
    )

    inputs = nn(tokens, shuffle)
    scale_in = inverse_rms(inputs)
    normed_in = inputs * scale_in
    own_in = normed_in.astype(narrow)
    both_in = jnp.concatenate([own_in, swap(own_in)], axis=0)
    own_cot = nn(cotangent, shuffle).astype(narrow)
    both_cot = jnp.concatenate([own_cot, swap(own_cot)], axis=0)
    cot_t = both_cot.T
    in_t = both_in.T

    proj_q = nn(both_in, full_q)
    proj_k = nn(both_in, full_k)
    proj_v = nn(both_in, full_v)
    proj_u = nn(both_in, full_u)
    query = jax.nn.silu(proj_q).astype(narrow)
    keys = jax.nn.silu(proj_k).astype(narrow)
    values = proj_v.astype(narrow)
    attended = per_head(attend_kernel, turn, decay_rates, (query, keys, values), (wide,))[0]

    def both_sum(part):
        other = swap(part)
        return part + jnp.concatenate([other[rows:], other[:rows]], axis=0)

    total_sq = both_sum(jnp.sum(attended * attended, axis=1))
    scale_out = lax.rsqrt(total_sq / width + eps)[:, None]
    normed_out = attended * scale_out
    gated = (normed_out * proj_u).astype(narrow)
    branch = nt(gated, full_o)
    middle = inputs + branch[:rows] + swap(branch[rows:])
    scale_mid = inverse_rms(middle)
    normed_mid = middle * scale_mid
    own_mid = normed_mid.astype(narrow)
    both_mid = jnp.concatenate([own_mid, swap(own_mid)], axis=0)
    mid_t = both_mid.T

    sums = None
    ffn_grads = []
    for c in range(len(cuts)):
        y_sum, d_sum, grads = ffn_chunk(
            both_mid, both_cot, mid_t, cot_t, gathered[5 + c], sums
        )
        sums = (y_sum, d_sum)
        ffn_grads.append(scatter(send, quarters(grads), c % 2 == 0))

    grad_mid_norm = d_sum[:rows] + swap(d_sum[rows:])
    grad_middle = own_cot.astype(wide) + norm_back(grad_mid_norm, normed_mid, scale_mid)
    own_e = grad_middle.astype(narrow)
    both_e = jnp.concatenate([own_e, swap(own_e)], axis=0)
    grad_gated = nn(both_e, full_o)
    grad_wout = tn(both_e, gated)
    attn_grads = [scatter(send, quarters(grad_wout), True)]
    grad_normed = grad_gated * proj_u
    grad_unit = (grad_gated * normed_out).astype(narrow)
    attn_grads.append(scatter(send, quarters(nn(in_t, grad_unit)), False))
    cross = both_sum(jnp.sum(grad_normed * normed_out, axis=1))
    grad_attended = (scale_out * (grad_normed - normed_out * (cross / width)[:, None])).astype(
        narrow
    )
    grad_q, grad_k, grad_v = per_head(
        attend_back_kernel,
        turn,
        decay_rates,
        (query, keys, values, grad_attended, proj_q, proj_k),
        (narrow, narrow, narrow),
    )
    attn_grads.append(scatter(send, quarters(nn(in_t, grad_q)), True))
    attn_grads.append(scatter(send, quarters(nn(in_t, grad_k)), False))
    attn_grads.append(scatter(send, quarters(nn(in_t, grad_v)), True))

    total = nt(grad_q, full_q) + nt(grad_k, full_k) + nt(grad_v, full_v) + nt(grad_unit, full_u)
    grad_in_norm = total[:rows] + swap(total[rows:])
    tokens_grad = grad_middle + norm_back(grad_in_norm, normed_in, scale_in)
    layer_out = (middle + y_sum[:rows] + swap(y_sum[rows:])).astype(narrow)
    layer_out = nt(layer_out, shuffle).astype(narrow)
    parts = []
    rest = tokens_grad
    for _ in range(3):
        part = lax.reduce_precision(rest, 8, 7)
        parts.append(part.astype(narrow))
        rest = rest - part
    tokens_grad = nt(parts[0], shuffle) + (nt(parts[1], shuffle) + nt(parts[2], shuffle))
    thirds = [
        jnp.concatenate([grad[:, i * n : (i + 1) * n] for grad, (_, n) in zip(ffn_grads, cuts)], axis=1)
        for i in range(3)
    ]
    return (
        layer_out,
        tokens_grad,
        attn_grads[2],
        attn_grads[3],
        attn_grads[4],
        attn_grads[1],
        attn_grads[0].T,
        thirds[0],
        thirds[1],
        thirds[2].T,
    )


def solution(mesh):
    return jax.shard_map(
        functools.partial(shards, mesh.shape["dp"]),
        mesh=mesh,
        in_specs=(
            P(("dp", "tensor"), None),
            P("dp", "tensor"),
            P("dp", "tensor"),
            P("dp", "tensor"),
            P("dp", "tensor"),
            P("tensor", "dp"),
            P("dp", "tensor"),
            P("dp", "tensor"),
            P("tensor", "dp"),
            P("tensor"),
            P(("dp", "tensor"), None),
        ),
        out_specs=(
            P(("dp", "tensor"), None),
            P(("dp", "tensor"), None),
            P("dp", "tensor"),
            P("dp", "tensor"),
            P("dp", "tensor"),
            P("dp", "tensor"),
            P("tensor", "dp"),
            P("dp", "tensor"),
            P("dp", "tensor"),
            P("tensor", "dp"),
        ),
        check_vma=False,
    )
```

```python
import functools

import jax
import jax.numpy as jnp
import numpy as np
from jax import lax
from jax.experimental import pallas as pl
from jax.experimental.pallas import tpu as pltpu
from jax.sharding import PartitionSpec as P

eps = 1e-06
wide = jnp.float32
narrow = jnp.bfloat16
in_flight = 6
per_link = 2
tile_width = 512


def dot(left, right, dims):
    return lax.dot_general(left, right, (dims, ((), ())), preferred_element_type=wide)


def nn(left, right):
    return dot(left, right, ((1,), (0,)))


def nt(left, right):
    return dot(left, right, ((1,), (1,)))


def tn(left, right):
    return dot(left, right, ((0,), (0,)))


def inverse_rms(values):
    return lax.rsqrt(jnp.mean(values * values, axis=-1, keepdims=True) + eps)


def norm_back(grad, normed, scale):
    return scale * (grad - normed * jnp.mean(grad * normed, axis=-1, keepdims=True))


def silu_slope(values):
    sigma = jax.nn.sigmoid(values)
    return sigma * (1.0 + values * (1.0 - sigma))


class Exchange:

    def __init__(self, size):
        self.size = size
        self.sent = []
        self.links = {1: [], 2: [], 4: []}

    def __call__(self, array, bit):
        link = self.links[min(bit, 4)]
        ahead = [q[-n] for q, n in ((self.sent, in_flight), (link, per_link)) if len(q) >= n]
        if ahead:
            array = lax.optimization_barrier((array, *ahead))[0]
        pairs = [(i, i ^ bit) for i in range(self.size)]
        result = lax.ppermute(array, "dp", pairs)
        self.sent.append(result)
        link.append(result)
        return result


def inner_bits(size):
    bits = []
    bit = size // 2
    while bit >= 4:
        bits.append(bit)
        bit //= 2
    return bits


def block_offsets(size):
    order = [0]
    for bit in inner_bits(size) + [1, 2]:
        order = order + [entry ^ bit for entry in order]
    return np.array(order, np.int32)


class Gather:

    def __init__(self, send, shard, turn):
        self.send = send
        self.held = shard
        self.turn = turn

    def inner(self, bit):
        self.held = jnp.concatenate([self.held, self.send(self.held, bit)], axis=0)

    def sides(self):
        self.side = self.send(self.held, 1)
        self.up = self.send(self.held, 2)

    def far(self):
        far = self.send(self.side, 2) if self.turn else self.send(self.up, 1)
        self.pieces = [self.held, self.side, self.up, far]


def low(value):
    return value.astype(narrow)


class Scatter:

    def __init__(self, send, pieces, turn):
        self.send = send
        self.first, self.side, self.up, self.away = pieces
        self.turn = turn

    def far(self):
        if self.turn:
            self.far_got = self.send(self.away, 2)
        else:
            self.far_got = self.send(self.away, 1)

    def near(self):
        if self.turn:
            self.near_got = self.send(self.up, 2)
        else:
            self.near_got = self.send(self.side, 1)

    def sides(self):
        rest = self.side if self.turn else self.up
        rest = low(rest.astype(wide) + self.far_got.astype(wide))
        got = self.send(rest, 1 if self.turn else 2)
        self.total = self.first.astype(wide) + self.near_got.astype(wide) + got.astype(wide)

    def inner(self, bit):
        half = self.total.shape[0] // 2
        got = self.send(low(self.total[half:]), bit)
        self.total = self.total[:half] + got.astype(wide)

    def rest(self):
        for bit in reversed(inner_bits(self.send.size)):
            self.inner(bit)


def tables(rate, size):
    row = lax.broadcasted_iota(jnp.int32, (size, 1), 0).astype(wide)
    col = lax.broadcasted_iota(jnp.int32, (1, size), 1).astype(wide)
    ahead = jnp.exp(-rate * row)
    inner = jnp.where(col <= row, ahead * jnp.exp(rate * col), 0.0)
    outof = jnp.exp(-rate * (size - row))
    return inner, ahead, outof


def attend_kernel(turn_ref, rate_ref, q_ref, k_ref, v_ref, o_ref):
    size = q_ref.shape[0] // 2
    inner, ahead, outof = tables(rate_ref[pl.program_id(0)], size)
    turn = turn_ref[0]
    early = pl.ds(pl.multiple_of(turn * size, size), size)
    late = pl.ds(pl.multiple_of((1 - turn) * size, size), size)

    def local(rows):
        weights = (nt(q_ref[rows, :], k_ref[rows, :]) * inner).astype(narrow)
        return nn(weights, v_ref[rows, :])

    weighted = (k_ref[early, :].astype(wide) * outof).astype(narrow)
    state = tn(weighted, v_ref[early, :]).astype(narrow)
    o_ref[early, :] = local(early)
    o_ref[late, :] = local(late) + nn(q_ref[late, :], state) * ahead


def per_head(kernel, turn, rates, arrays, out_types):
    heads = rates.shape[0]
    length, columns = arrays[0].shape
    spec = pl.BlockSpec((length, columns // heads), lambda h: (0, h))
    scalar = pl.BlockSpec(memory_space=pltpu.SMEM)
    return pl.pallas_call(
        kernel,
        grid=(heads,),
        in_specs=[scalar, scalar] + [spec] * len(arrays),
        out_specs=[spec] * len(out_types),
        out_shape=[jax.ShapeDtypeStruct((length, columns), t) for t in out_types],
    )(turn, rates, *arrays)


def rows_of(refs):
    half = refs[0].shape[0]
    return [(ref, slice(i * half, (i + 1) * half)) for i, ref in enumerate(refs)]


def project_kernel(own_ref, other_ref, w0, w1, w2, w3, *outs, form):
    weight = jnp.concatenate([ref[...] for ref in (w0, w1, w2, w3)], axis=0)
    for ref, rows in rows_of((own_ref, other_ref)):
        value = nn(ref[...], weight)
        if form == "silu":
            outs[0][rows, :] = value
            outs[1][rows, :] = jax.nn.silu(value).astype(narrow)
        else:
            outs[0][rows, :] = value.astype(outs[0].dtype)


def project(pair, pieces, form):
    rows = pair[0].shape[0]
    length, width = 2 * rows, pieces[0].shape[1]
    types = {"silu": (wide, narrow), "wide": (wide,), "narrow": (narrow,)}[form]
    return pl.pallas_call(
        functools.partial(project_kernel, form=form),
        out_shape=[jax.ShapeDtypeStruct((length, width), t) for t in types],
    )(*pair, *pieces)


def branch_kernel(o_ref, scale_ref, u_ref, w0, w1, w2, w3, gated_ref, own_ref, other_ref):
    rows = own_ref.shape[0]
    quarter = w0.shape[0]
    for half, out in ((slice(0, rows), own_ref), (slice(rows, 2 * rows), other_ref)):
        gated = (o_ref[half, :] * scale_ref[half, :] * u_ref[half, :]).astype(narrow)
        gated_ref[half, :] = gated
        for i, ref in enumerate((w0, w1, w2, w3)):
            out[:, i * quarter : (i + 1) * quarter] = nt(gated, ref[...]).astype(out.dtype)


def branch(attended, scale, proj_u, pieces):
    length, heads = attended.shape
    rows, width = length // 2, 4 * pieces[0].shape[0]
    return pl.pallas_call(
        branch_kernel,
        out_shape=[
            jax.ShapeDtypeStruct((length, heads), narrow),
            jax.ShapeDtypeStruct((rows, width), wide),
            jax.ShapeDtypeStruct((rows, width), narrow),
        ],
    )(attended, scale, proj_u, *pieces)


def unbranch_kernel(
    own_ref, other_ref, o_ref, scale_ref, u_ref, w0, w1, w2, w3, grad_ref, unit_ref, cross_ref
):
    weight = jnp.concatenate([ref[...] for ref in (w0, w1, w2, w3)], axis=0)
    for ref, rows in rows_of((own_ref, other_ref)):
        value = nn(ref[...], weight)
        normed = o_ref[rows, :] * scale_ref[rows, :]
        unit_ref[rows, :] = (value * normed).astype(narrow)
        value = value * u_ref[rows, :]
        grad_ref[rows, :] = value
        cross_ref[rows, :] = jnp.sum(value * normed, axis=1, keepdims=True)


def unbranch(pair, attended, scale, proj_u, pieces):
    length, heads = attended.shape
    return pl.pallas_call(
        unbranch_kernel,
        out_shape=[
            jax.ShapeDtypeStruct((length, heads), wide),
            jax.ShapeDtypeStruct((length, heads), narrow),
            jax.ShapeDtypeStruct((length, 1), wide),
        ],
    )(*pair, attended, scale, proj_u, *pieces)


def attend_back_kernel(
    turn_ref,
    rate_ref,
    scale_ref,
    cross_ref,
    q_ref,
    k_ref,
    v_ref,
    pq_ref,
    pk_ref,
    gn_ref,
    o_ref,
    dq_ref,
    dk_ref,
    dv_ref,
    g_ref,
):
    size = q_ref.shape[0] // 2
    inner, ahead, outof = tables(rate_ref[pl.program_id(0)], size)
    turn = turn_ref[0]
    early = pl.ds(pl.multiple_of(turn * size, size), size)
    late = pl.ds(pl.multiple_of((1 - turn) * size, size), size)
    scale = scale_ref[...]
    normed = o_ref[...] * scale
    g_ref[...] = (scale * (gn_ref[...] - normed * cross_ref[...])).astype(narrow)

    def local(rows):
        q, k, v, g = (ref[rows, :] for ref in (q_ref, k_ref, v_ref, g_ref))
        weights = (nt(q, k) * inner).astype(narrow)
        grad_scores = (nt(g, v) * inner).astype(narrow)
        return nn(grad_scores, k), tn(grad_scores, q), tn(weights, g)

    def store(rows, dq, dk, dv):
        dq_ref[rows, :] = (dq * silu_slope(pq_ref[rows, :])).astype(narrow)
        dk_ref[rows, :] = (dk * silu_slope(pk_ref[rows, :])).astype(narrow)
        dv_ref[rows, :] = dv.astype(narrow)

    weighted = (k_ref[early, :].astype(wide) * outof).astype(narrow)
    state = tn(weighted, v_ref[early, :]).astype(narrow)
    g_ahead = (g_ref[late, :].astype(wide) * ahead).astype(narrow)
    grad_state = tn(q_ref[late, :], g_ahead).astype(narrow)
    dq, dk, dv = local(late)
    store(late, dq + nt(g_ahead, state), dk, dv)
    dq, dk, dv = local(early)
    store(
        early,
        dq,
        dk + nt(v_ref[early, :], grad_state) * outof,
        dv + nn(weighted, grad_state),
    )


def attend_back(turn, rates, scale, cross, arrays):
    heads = rates.shape[0]
    length, columns = arrays[0].shape
    spec = pl.BlockSpec((length, columns // heads), lambda h: (0, h))
    column = pl.BlockSpec((length, 1), lambda h: (0, 0))
    scalar = pl.BlockSpec(memory_space=pltpu.SMEM)
    return pl.pallas_call(
        attend_back_kernel,
        grid=(heads,),
        in_specs=[scalar, scalar, column, column] + [spec] * len(arrays),
        out_specs=[spec] * 3,
        out_shape=[jax.ShapeDtypeStruct((length, columns), narrow)] * 3,
        scratch_shapes=[pltpu.VMEM((length, columns // heads), narrow)],
    )(turn, rates, scale, cross, *arrays)


def weight_grad_kernel(own_ref, other_ref, *refs):
    count = len(refs) // 2
    for z_ref, out in zip(refs[:count], refs[count:]):
        total = 0.0
        for ref, rows in rows_of((own_ref, other_ref)):
            total += tn(ref[...], z_ref[rows, :])
        out[0] = total.astype(narrow)


def weight_grads(pair, arrays):
    rows, width = pair[0].shape
    quarter = width // 4
    columns = arrays[0].shape[1]
    part = pl.BlockSpec((rows, quarter), lambda i: (0, i))
    whole = pl.BlockSpec((2 * rows, columns), lambda i: (0, 0))
    outs = pl.pallas_call(
        weight_grad_kernel,
        grid=(4,),
        in_specs=[part] * 2 + [whole] * len(arrays),
        out_specs=[pl.BlockSpec((1, quarter, columns), lambda i: (i, 0, 0))] * len(arrays),
        out_shape=[jax.ShapeDtypeStruct((4, quarter, columns), narrow)] * len(arrays),
    )(*pair, *arrays)
    return [[out[i] for i in range(4)] for out in outs]


def ffn_kernel(*refs, count, chained, last):
    n_refs, g_refs = refs[0:2], refs[2:4]
    refs = refs[4:]
    piece_refs = [refs[4 * i : 4 * i + 4] for i in range(count)]
    refs = refs[4 * count :]
    if chained:
        befores, refs = refs[:4], refs[4:]
    sums, refs = refs[:4], refs[4:]
    grad_refs = [refs[4 * i : 4 * i + 4] for i in range(count)]
    w_ref, s_ref, d_ref = refs[4 * count : 4 * count + 3]
    accs = refs[4 * count + 3 :]
    rows = n_refs[0].shape[0]
    quarter = w_ref.shape[0] // 4
    n = s_ref.shape[1]

    for c in range(count):
        for i, ref in enumerate(piece_refs[c]):
            w_ref[i * quarter : (i + 1) * quarter, :] = ref[...]
        for h in range(2):
            half = slice(h * rows, (h + 1) * rows)
            ab = nn(n_refs[h][...], w_ref[:, : 2 * n])
            ds = nn(g_refs[h][...], w_ref[:, 2 * n :])
            a = ab[:, :n]
            b = ab[:, n:]
            s_ref[half, :] = (a * b).astype(narrow)
            d_ref[half, :n] = (ds * b).astype(narrow)
            d_ref[half, n:] = (ds * a).astype(narrow)
            y = nt(s_ref[half, :], w_ref[:, 2 * n :])
            d = nt(d_ref[half, :], w_ref[:, : 2 * n])
            for value, k in ((y, h), (d, 2 + h)):
                if c > 0:
                    value = value + accs[k][...]
                elif chained:
                    value = value + befores[k][...]
                if c == count - 1:
                    sums[k][...] = value.astype(sums[k].dtype)
                else:
                    accs[k][...] = value
        for i in range(4):
            cols = slice(i * quarter, (i + 1) * quarter)
            out = grad_refs[c][i]
            out[:, : 2 * n] = sum(
                tn(n_refs[h][:, cols], d_ref[h * rows : (h + 1) * rows, :]) for h in range(2)
            ).astype(narrow)
            out[:, 2 * n :] = sum(
                tn(g_refs[h][:, cols], s_ref[h * rows : (h + 1) * rows, :]) for h in range(2)
            ).astype(narrow)


def ffn(normed, grad, tiles, sums, last):
    rows, width = normed[0].shape
    count = len(tiles)
    quarter, n3 = tiles[0][0].shape
    n = n3 // 3
    flat = [piece for pieces in tiles for piece in pieces]
    other = narrow if last else wide
    types = [wide, other, wide, other]
    outs = pl.pallas_call(
        functools.partial(ffn_kernel, count=count, chained=sums is not None, last=last),
        out_shape=[jax.ShapeDtypeStruct((rows, width), t) for t in types]
        + [jax.ShapeDtypeStruct((quarter, n3), narrow)] * (4 * count),
        scratch_shapes=[
            pltpu.VMEM((width, n3), narrow),
            pltpu.VMEM((2 * rows, n), narrow),
            pltpu.VMEM((2 * rows, 2 * n), narrow),
        ]
        + [pltpu.VMEM((rows, width), wide)] * (4 if count > 1 else 0),
    )(*normed, *grad, *flat, *(sums or ()))
    return outs[:4], [outs[4 + 4 * i : 8 + 4 * i] for i in range(count)]


def ffn_cuts(total):
    cuts = []
    left = total
    while left > 0:
        take = min(tile_width, left)
        cuts.append((total - left, take))
        left -= take
    return cuts


def shards(
    size,
    tokens,
    w_query,
    w_key,
    w_value,
    w_gate,
    w_out,
    w_first,
    w_second,
    w_down,
    decay_rates,
    cotangent,
):
    send = Exchange(size)
    swap = lambda value: lax.ppermute(value, "tensor", [(0, 1), (1, 0)])
    me = lax.axis_index("dp")
    turn = lax.axis_index("tensor").astype(jnp.int32).reshape(1)
    rows, width = tokens.shape
    span = width // size
    offsets = jnp.asarray(np.repeat(block_offsets(size), span))
    place = jnp.bitwise_xor(offsets, me) * span + jnp.arange(width) % span
    shuffle = (jnp.arange(width)[:, None] == place[None, :]).astype(narrow)

    cuts = ffn_cuts(w_first.shape[1])
    down_t = w_down.T
    att = [
        Gather(send, w, i % 2 == 0)
        for i, w in enumerate((w_query, w_key, w_value, w_gate, w_out.T))
    ]
    mlp = [
        Gather(
            send,
            jnp.concatenate([w[:, at : at + n] for w in (w_first, w_second, down_t)], axis=1),
            i % 2 == 0,
        )
        for i, (at, n) in enumerate(cuts)
    ]
    bits = inner_bits(size)
    for step in range(len(att) + len(bits) + 1):
        c = step - len(bits) - 1
        if 0 <= c < len(att):
            att[c].far()
        c = step - len(bits)
        if 0 <= c < len(att):
            att[c].sides()
        for level in range(len(bits) - 1, -1, -1):
            c = step - level
            if 0 <= c < len(att):
                att[c].inner(bits[level])
            elif len(att) <= c < len(att) + len(mlp):
                mlp[c - len(att)].inner(bits[level])
    step = len(att) + len(bits) + 1
    for level in range(len(bits)):
        for c in range(max(0, step - level - len(att)), len(mlp)):
            mlp[c].inner(bits[level])
    for c in range(len(mlp) + 1):
        if c < len(mlp):
            mlp[c].sides()
        if c > 0:
            mlp[c - 1].far()
    full_q, full_k, full_v, full_u, full_o = (gather.pieces for gather in att)

    inputs = nn(tokens, shuffle)
    scale_in = inverse_rms(inputs)
    normed_in = inputs * scale_in
    own_in = low(normed_in)
    pair_in = (own_in, swap(own_in))
    own_cot = low(nn(cotangent, shuffle))
    pair_cot = (own_cot, swap(own_cot))

    proj_q, query = project(pair_in, full_q, "silu")
    proj_k, keys = project(pair_in, full_k, "silu")
    values = project(pair_in, full_v, "narrow")[0]
    proj_u = project(pair_in, full_u, "wide")[0]
    attended = per_head(attend_kernel, turn, decay_rates, (query, keys, values), (wide,))[0]

    def both_sum(part):
        other = swap(part)
        return part + jnp.concatenate([other[rows:], other[:rows]], axis=0)

    total_sq = both_sum(jnp.sum(attended * attended, axis=1))
    scale_out = lax.rsqrt(total_sq / width + eps)[:, None]
    gated, branch_own, branch_other = branch(attended, scale_out, proj_u, full_o)
    middle = inputs + branch_own + swap(branch_other).astype(wide)
    scale_mid = inverse_rms(middle)
    normed_mid = middle * scale_mid
    own_mid = low(normed_mid)
    pair_mid = (own_mid, swap(own_mid))

    tiles = [gather.pieces for gather in mlp]
    sums, grads = ffn(pair_mid, pair_cot, tiles[:-1], None, False)
    outs = [Scatter(send, grad, i % 2 == 0) for i, grad in enumerate(grads)]
    for stage in (Scatter.far, Scatter.near, Scatter.sides):
        for out in outs:
            stage(out)
    (y_own, y_other, d_own, d_other), grads = ffn(pair_mid, pair_cot, tiles[-1:], sums, True)
    outs.append(Scatter(send, grads[0], len(outs) % 2 == 0))
    for stage in (Scatter.far, Scatter.near, Scatter.sides):
        stage(outs[-1])
    for out in outs:
        out.rest()

    grad_mid_norm = d_own + swap(d_other).astype(wide)
    grad_middle = own_cot.astype(wide) + norm_back(grad_mid_norm, normed_mid, scale_mid)
    own_e = low(grad_middle)
    pair_e = (own_e, swap(own_e))
    grad_normed, grad_unit, cross = unbranch(pair_e, attended, scale_out, proj_u, full_o)
    cross = both_sum(cross[:, 0]) / width
    late = [
        Scatter(send, weight_grads(pair_e, (gated,))[0], True),
        Scatter(send, weight_grads(pair_in, (grad_unit,))[0], False),
    ]
    for stage in (Scatter.far, Scatter.near, Scatter.sides):
        for out in late:
            stage(out)
    grad_q, grad_k, grad_v = attend_back(
        turn,
        decay_rates,
        scale_out,
        cross[:, None],
        (query, keys, values, proj_q, proj_k, grad_normed, attended),
    )
    last = [
        Scatter(send, grad, i % 2 == 0)
        for i, grad in enumerate(weight_grads(pair_in, (grad_q, grad_k, grad_v)))
    ]
    for stage in (Scatter.far, Scatter.near, Scatter.sides):
        for out in last:
            stage(out)
    for out in late + last:
        out.rest()

    join = lambda pieces: jnp.concatenate(pieces, axis=0)
    total = nt(grad_q, join(full_q)) + nt(grad_k, join(full_k))
    total = total + (nt(grad_v, join(full_v)) + nt(grad_unit, join(full_u)))
    grad_in_norm = total[:rows] + swap(low(total[rows:])).astype(wide)
    tokens_grad = grad_middle + norm_back(grad_in_norm, normed_in, scale_in)
    layer_out = low(middle + y_own + swap(y_other).astype(wide))
    layer_out = low(nt(layer_out, shuffle))
    parts = []
    rest = tokens_grad
    for _ in range(3):
        part = lax.reduce_precision(rest, 8, 7)
        parts.append(low(part))
        rest = rest - part
    tokens_grad = nt(parts[0], shuffle) + (nt(parts[1], shuffle) + nt(parts[2], shuffle))
    thirds = [
        jnp.concatenate(
            [out.total[:, i * n : (i + 1) * n] for out, (_, n) in zip(outs, cuts)], axis=1
        )
        for i in range(3)
    ]
    return (
        layer_out,
        tokens_grad,
        last[0].total,
        last[1].total,
        last[2].total,
        late[1].total,
        late[0].total.T,
        thirds[0],
        thirds[1],
        thirds[2].T,
    )


def solution(mesh):
    return jax.shard_map(
        functools.partial(shards, mesh.shape["dp"]),
        mesh=mesh,
        in_specs=(
            P(("dp", "tensor"), None),
            P("dp", "tensor"),
            P("dp", "tensor"),
            P("dp", "tensor"),
            P("dp", "tensor"),
            P("tensor", "dp"),
            P("dp", "tensor"),
            P("dp", "tensor"),
            P("tensor", "dp"),
            P("tensor"),
            P(("dp", "tensor"), None),
        ),
        out_specs=(
            P(("dp", "tensor"), None),
            P(("dp", "tensor"), None),
            P("dp", "tensor"),
            P("dp", "tensor"),
            P("dp", "tensor"),
            P("dp", "tensor"),
            P("tensor", "dp"),
            P("dp", "tensor"),
            P("dp", "tensor"),
            P("tensor", "dp"),
        ),
        check_vma=False,
    )
```

```python
import functools

import jax
import jax.numpy as jnp
import numpy as np
from jax import lax
from jax.experimental import pallas as pl
from jax.experimental.pallas import tpu as pltpu
from jax.sharding import PartitionSpec as P

eps = 1e-06
wide = jnp.float32
narrow = jnp.bfloat16
in_flight = 6
per_link = 2
tile_width = 512


def dot(left, right, dims):
    return lax.dot_general(left, right, (dims, ((), ())), preferred_element_type=wide)


def nn(left, right):
    return dot(left, right, ((1,), (0,)))


def nt(left, right):
    return dot(left, right, ((1,), (1,)))


def tn(left, right):
    return dot(left, right, ((0,), (0,)))


def inverse_rms(values):
    return lax.rsqrt(jnp.mean(values * values, axis=-1, keepdims=True) + eps)


def norm_back(grad, normed, scale):
    return scale * (grad - normed * jnp.mean(grad * normed, axis=-1, keepdims=True))


class Exchange:

    def __init__(self, size):
        self.size = size
        self.sent = []
        self.links = {1: [], 2: [], 4: []}

    def __call__(self, array, bit):
        link = self.links[min(bit, 4)]
        ahead = [q[-n] for q, n in ((self.sent, in_flight), (link, per_link)) if len(q) >= n]
        if ahead:
            array = lax.optimization_barrier((array, *ahead))[0]
        pairs = [(i, i ^ bit) for i in range(self.size)]
        result = lax.ppermute(array, "dp", pairs)
        self.sent.append(result)
        link.append(result)
        return result


def inner_bits(size):
    bits = []
    bit = size // 2
    while bit >= 4:
        bits.append(bit)
        bit //= 2
    return bits


def block_offsets(size):
    order = [0]
    for bit in inner_bits(size) + [1, 2]:
        order = order + [entry ^ bit for entry in order]
    return np.array(order, np.int32)


class Gather:

    def __init__(self, send, shard, turn):
        self.send = send
        self.held = shard
        self.turn = turn

    def inner(self, bit):
        self.held = jnp.concatenate([self.held, self.send(self.held, bit)], axis=0)

    def sides(self):
        self.side = self.send(self.held, 1)
        self.up = self.send(self.held, 2)

    def far(self):
        far = self.send(self.side, 2) if self.turn else self.send(self.up, 1)
        self.pieces = [self.held, self.side, self.up, far]


def low(value):
    return value.astype(narrow)


class Scatter:

    def __init__(self, send, pieces, turn):
        self.send = send
        self.first, self.side, self.up, self.away = pieces
        self.turn = turn

    def far(self):
        if self.turn:
            self.far_got = self.send(self.away, 2)
        else:
            self.far_got = self.send(self.away, 1)

    def near(self):
        if self.turn:
            self.near_got = self.send(self.up, 2)
        else:
            self.near_got = self.send(self.side, 1)

    def sides(self):
        rest = self.side if self.turn else self.up
        rest = low(rest.astype(wide) + self.far_got.astype(wide))
        got = self.send(rest, 1 if self.turn else 2)
        self.total = self.first.astype(wide) + self.near_got.astype(wide) + got.astype(wide)

    def inner(self, bit):
        half = self.total.shape[0] // 2
        got = self.send(low(self.total[half:]), bit)
        self.total = self.total[:half] + got.astype(wide)

    def rest(self):
        for bit in reversed(inner_bits(self.send.size)):
            self.inner(bit)


def tables(rate, size):
    row = lax.broadcasted_iota(jnp.int32, (size, 1), 0).astype(wide)
    col = lax.broadcasted_iota(jnp.int32, (1, size), 1).astype(wide)
    ahead = jnp.exp(-rate * row)
    inner = jnp.where(col <= row, ahead * jnp.exp(rate * col), 0.0)
    outof = jnp.exp(-rate * (size - row))
    return inner, ahead, outof


def cost(flops, *arrays):
    size = sum(a.size * jnp.dtype(a.dtype).itemsize for a in arrays)
    return pl.CostEstimate(flops=int(flops), transcendentals=0, bytes_accessed=int(size))


def rows_of(refs):
    half = refs[0].shape[0]
    return [(ref, slice(i * half, (i + 1) * half)) for i, ref in enumerate(refs)]


def join(refs):
    return jnp.concatenate([ref[...] for ref in refs], axis=0)


def row_sums(values):
    ones = jnp.ones((8, values.shape[1]), wide)
    return lax.dot_general(
        ones,
        values,
        (((1,), (1,)), ((), ())),
        precision=lax.Precision.HIGHEST,
        preferred_element_type=wide,
    )


def column(own, other):
    half = own.shape[1] // 2
    total = own + jnp.concatenate([other[:, half:], other[:, :half]], axis=1)
    return jnp.transpose(total)[:, :1]


def spans(turn_ref, size):
    turn = turn_ref[0]
    early = pl.ds(pl.multiple_of(turn * size, size), size)
    late = pl.ds(pl.multiple_of((1 - turn) * size, size), size)
    return early, late


def front_kernel(turn_ref, rate_ref, own_ref, other_ref, *refs, heads):
    wq, wk, wv = refs[0:4], refs[4:8], refs[8:12]
    q_ref, k_ref, v_ref, sq_ref, sk_ref, o_ref, sum_ref = refs[12:]
    pair = rows_of((own_ref, other_ref))
    for pieces, out, slope in ((wq, q_ref, sq_ref), (wk, k_ref, sk_ref)):
        weight = join(pieces)
        for ref, rows in pair:
            value = nn(ref[...], weight)
            sigma = jax.nn.sigmoid(value)
            out[rows, :] = low(value * sigma)
            slope[rows, :] = low(sigma * (1.0 + value * (1.0 - sigma)))
    weight = join(wv)
    for ref, rows in pair:
        v_ref[rows, :] = low(nn(ref[...], weight))
    size = own_ref.shape[0]
    early, late = spans(turn_ref, size)
    wide_head = q_ref.shape[1] // heads
    sums = 0.0
    for j in range(heads):
        cols = slice(j * wide_head, (j + 1) * wide_head)
        inner, ahead, outof = tables(rate_ref[pl.program_id(0) * heads + j], size)

        def local(rows):
            weights = low(nt(q_ref[rows, cols], k_ref[rows, cols]) * inner)
            return nn(weights, v_ref[rows, cols])

        weighted = low(k_ref[early, cols].astype(wide) * outof)
        state = low(tn(weighted, v_ref[early, cols]))
        o_ref[early, cols] = local(early)
        o_ref[late, cols] = local(late) + nn(q_ref[late, cols], state) * ahead
    values = o_ref[...]
    sums = row_sums(values * values)

    @pl.when(pl.program_id(0) == 0)
    def _():
        sum_ref[...] = sums

    @pl.when(pl.program_id(0) > 0)
    def _():
        sum_ref[...] += sums


def front(turn, rates, pair, pieces):
    rows, width = pair[0].shape
    quarter, columns = pieces[0][0].shape
    steps = 2
    block = columns // steps
    scalar = pl.BlockSpec(memory_space=pltpu.SMEM)
    whole = lambda shape: pl.BlockSpec(shape, lambda i: (0, 0))
    piece = pl.BlockSpec((quarter, block), lambda i: (0, i))
    out = pl.BlockSpec((2 * rows, block), lambda i: (0, i))
    types = [narrow] * 5 + [wide]
    return pl.pallas_call(
        functools.partial(front_kernel, heads=rates.shape[0] // steps),
        cost_estimate=cost(18 * rows * width * columns, *pair, *pair, *pair, *pair, *pair),
        grid=(steps,),
        in_specs=[scalar, scalar] + [whole((rows, width))] * 2 + [piece] * 12,
        out_specs=[out] * 6 + [whole((8, 2 * rows))],
        out_shape=[jax.ShapeDtypeStruct((2 * rows, columns), t) for t in types]
        + [jax.ShapeDtypeStruct((8, 2 * rows), wide)],
    )(turn, rates, *pair, *(p for ps in pieces for p in ps))


def gate_kernel(own_ref, other_ref, w0, w1, w2, w3, u_ref):
    weight = join((w0, w1, w2, w3))
    for ref, rows in rows_of((own_ref, other_ref)):
        u_ref[rows, :] = nn(ref[...], weight).astype(u_ref.dtype)


def gate(pair, pieces):
    rows = pair[0].shape[0]
    return pl.pallas_call(
        gate_kernel,
        cost_estimate=cost(4 * rows * pieces[0].size * 4, *pair, *pair),
        out_shape=jax.ShapeDtypeStruct((2 * rows, pieces[0].shape[1]), wide),
    )(*pair, *pieces)


def branch_kernel(
    sum_ref, got_ref, o_ref, u_ref, w0, w1, w2, w3, gated_ref, scale_ref, own_ref, other_ref
):
    rows = own_ref.shape[0]
    quarter = w0.shape[0]
    scale = lax.rsqrt(column(sum_ref[...], got_ref[...]) / (4 * quarter) + eps)
    scale_ref[...] = scale
    gated_ref[...] = low(o_ref[...] * scale * u_ref[...])
    for i, ref in enumerate((w0, w1, w2, w3)):
        cols = slice(i * quarter, (i + 1) * quarter)
        value = nt(gated_ref[...], ref[...])
        own_ref[:, cols] = value[:rows]
        other_ref[:, cols] = low(value[rows:])


def branch(sums, got, attended, proj_u, pieces):
    length, heads = attended.shape
    rows, width = length // 2, 4 * pieces[0].shape[0]
    return pl.pallas_call(
        branch_kernel,
        cost_estimate=cost(2 * length * heads * width, attended, attended, attended, proj_u),
        out_shape=[
            jax.ShapeDtypeStruct((length, heads), narrow),
            jax.ShapeDtypeStruct((length, 1), wide),
            jax.ShapeDtypeStruct((rows, width), wide),
            jax.ShapeDtypeStruct((rows, width), narrow),
        ],
    )(sums, got, attended, proj_u, *pieces)


def unbranch_kernel(
    own_ref, other_ref, o_ref, scale_ref, u_ref, w0, w1, w2, w3, grad_ref, unit_ref, cross_ref
):
    weight = join((w0, w1, w2, w3))
    for ref, rows in rows_of((own_ref, other_ref)):
        value = nn(ref[...], weight)
        normed = o_ref[rows, :] * scale_ref[rows, :]
        unit_ref[rows, :] = low(value * normed)
        value = value * u_ref[rows, :]
        grad_ref[rows, :] = value
        cross_ref[:, rows] = row_sums(value * normed)


def unbranch(pair, attended, scale, proj_u, pieces):
    length, heads = attended.shape
    width = pair[0].shape[1]
    return pl.pallas_call(
        unbranch_kernel,
        cost_estimate=cost(2 * length * heads * width, attended, attended, attended, proj_u),
        out_shape=[
            jax.ShapeDtypeStruct((length, heads), wide),
            jax.ShapeDtypeStruct((length, heads), narrow),
            jax.ShapeDtypeStruct((8, length), wide),
        ],
    )(*pair, attended, scale, proj_u, *pieces)


def attend_back_kernel(
    turn_ref,
    rate_ref,
    scale_ref,
    cross_ref,
    got_ref,
    q_ref,
    k_ref,
    v_ref,
    sq_ref,
    sk_ref,
    gn_ref,
    o_ref,
    dq_ref,
    dk_ref,
    dv_ref,
    g_ref,
    c_ref,
    *,
    width,
):
    size = q_ref.shape[0] // 2
    inner, ahead, outof = tables(rate_ref[pl.program_id(0)], size)
    early, late = spans(turn_ref, size)

    @pl.when(pl.program_id(0) == 0)
    def _():
        c_ref[...] = column(cross_ref[...], got_ref[...]) / width

    scale = scale_ref[...]
    normed = o_ref[...] * scale
    g_ref[...] = low(scale * (gn_ref[...] - normed * c_ref[...]))

    def local(rows):
        q, k, v, g = (ref[rows, :] for ref in (q_ref, k_ref, v_ref, g_ref))
        weights = low(nt(q, k) * inner)
        grad_scores = low(nt(g, v) * inner)
        return nn(grad_scores, k), tn(grad_scores, q), tn(weights, g)

    def store(rows, dq, dk, dv):
        dq_ref[rows, :] = low(dq * sq_ref[rows, :].astype(wide))
        dk_ref[rows, :] = low(dk * sk_ref[rows, :].astype(wide))
        dv_ref[rows, :] = low(dv)

    weighted = low(k_ref[early, :].astype(wide) * outof)
    state = low(tn(weighted, v_ref[early, :]))
    g_ahead = low(g_ref[late, :].astype(wide) * ahead)
    grad_state = low(tn(q_ref[late, :], g_ahead))
    dq, dk, dv = local(late)
    store(late, dq + nt(g_ahead, state), dk, dv)
    dq, dk, dv = local(early)
    store(
        early,
        dq,
        dk + nt(v_ref[early, :], grad_state) * outof,
        dv + nn(weighted, grad_state),
    )


def attend_back(turn, rates, scale, cross, got, arrays, width):
    heads = rates.shape[0]
    length, columns = arrays[0].shape
    spec = pl.BlockSpec((length, columns // heads), lambda h: (0, h))
    col = pl.BlockSpec((length, 1), lambda h: (0, 0))
    row = pl.BlockSpec((8, length), lambda h: (0, 0))
    scalar = pl.BlockSpec(memory_space=pltpu.SMEM)
    return pl.pallas_call(
        functools.partial(attend_back_kernel, width=width),
        cost_estimate=cost(12 * length * length * columns, *arrays, *arrays, *arrays),
        grid=(heads,),
        in_specs=[scalar, scalar, col, row, row] + [spec] * len(arrays),
        out_specs=[spec] * 3,
        out_shape=[jax.ShapeDtypeStruct((length, columns), narrow)] * 3,
        scratch_shapes=[
            pltpu.VMEM((length, columns // heads), narrow),
            pltpu.VMEM((length, 1), wide),
        ],
    )(turn, rates, scale, cross, got, *arrays)


def weight_grad_kernel(own_ref, other_ref, *refs):
    count = len(refs) // 5
    pair = rows_of((own_ref, other_ref))
    quarter = refs[count].shape[0]
    for j in range(count):
        for i in range(4):
            cols = slice(i * quarter, (i + 1) * quarter)
            total = sum(tn(ref[:, cols], refs[j][rows, :]) for ref, rows in pair)
            refs[count + 4 * j + i][...] = low(total)


def weight_grads(pair, arrays):
    rows, width = pair[0].shape
    columns = arrays[0].shape[1]
    outs = pl.pallas_call(
        weight_grad_kernel,
        cost_estimate=cost(4 * rows * width * columns * len(arrays), *pair, *arrays, *arrays),
        out_shape=[jax.ShapeDtypeStruct((width // 4, columns), narrow)] * (4 * len(arrays)),
    )(*pair, *arrays)
    return [outs[4 * j : 4 * j + 4] for j in range(len(arrays))]


def input_grad_kernel(*refs):
    grads, pieces, (own_ref, other_ref) = refs[:4], refs[4:20], refs[20:]
    quarter = pieces[0].shape[0]
    rows = own_ref.shape[0]
    for i in range(4):
        cols = slice(i * quarter, (i + 1) * quarter)
        value = sum(nt(grads[j][...], pieces[4 * j + i][...]) for j in range(4))
        own_ref[:, cols] = value[:rows]
        other_ref[:, cols] = low(value[rows:])


def input_grad(grads, pieces):
    length, columns = grads[0].shape
    rows, width = length // 2, 4 * pieces[0][0].shape[0]
    return pl.pallas_call(
        input_grad_kernel,
        cost_estimate=cost(8 * length * columns * width, *grads, *grads, *grads),
        out_shape=[
            jax.ShapeDtypeStruct((rows, width), wide),
            jax.ShapeDtypeStruct((rows, width), narrow),
        ],
    )(*grads, *(p for ps in pieces for p in ps))


def ffn_kernel(*refs, count):
    n_in, g_in = refs[0:2], refs[2:4]
    w_in = [refs[4 + 4 * c : 8 + 4 * c] for c in range(count)]
    refs = refs[4 + 4 * count :]
    sums_out = refs[0:4]
    o_out = [refs[4 + 4 * c : 8 + 4 * c] for c in range(count)]
    n_ref, g_ref, w_ref, s_ref, d_ref, acc_ref, low_ref, o_ref, in_sem, out_sem = refs[
        4 + 4 * count :
    ]
    rows = n_ref.shape[1]
    quarter = w_ref.shape[1] // 4
    n = s_ref.shape[2]
    part = lambda i: slice(i * quarter, (i + 1) * quarter)

    ready = [pltpu.make_async_copy(n_in[h], n_ref.at[h], in_sem.at[h]) for h in range(2)]
    ready += [pltpu.make_async_copy(g_in[h], g_ref.at[h], in_sem.at[2 + h]) for h in range(2)]
    load = [
        [
            pltpu.make_async_copy(
                w_in[c][i], w_ref.at[c, part(i), :], in_sem.at[4 + 4 * c + i]
            )
            for i in range(4)
        ]
        for c in range(count)
    ]
    for copy in load[0] + ready:
        copy.start()
    for copies in load[1:]:
        for copy in copies:
            copy.start()
    for copy in load[0] + ready:
        copy.wait()
    stores = []
    for c in range(count):
        if c > 0:
            for copy in load[c]:
                copy.wait()

        def half(h, carry, c=c):
            ab = nn(n_ref[h], w_ref[c, :, : 2 * n])
            ds = nn(g_ref[h], w_ref[c, :, 2 * n :])
            a = ab[:, :n]
            b = ab[:, n:]
            s_ref[h] = low(a * b)
            d_ref[h, :, :n] = low(ds * b)
            d_ref[h, :, n:] = low(ds * a)
            return carry

        lax.fori_loop(0, 2, half, 0)
        y = nt(s_ref[...].reshape(2 * rows, n), w_ref[c, :, 2 * n :]).reshape(2, rows, -1)
        d = nt(d_ref[...].reshape(2 * rows, 2 * n), w_ref[c, :, : 2 * n]).reshape(2, rows, -1)
        if c == 0:
            acc_ref[0] = y
            acc_ref[1] = d
        else:
            acc_ref[0] += y
            acc_ref[1] += d
        if c == count - 1:
            for k in range(2):
                low_ref[k] = low(acc_ref[k, 1])
                for at, source in ((2 * k, acc_ref.at[k, 0]), (2 * k + 1, low_ref.at[k])):
                    copy = pltpu.make_async_copy(source, sums_out[at], out_sem.at[at])
                    copy.start()
                    stores.append(copy)
        for i in (3, 2, 1, 0):
            o_ref[c, part(i), : 2 * n] = low(
                sum(tn(n_ref[h, :, part(i)], d_ref[h]) for h in range(2))
            )
            o_ref[c, part(i), 2 * n :] = low(
                sum(tn(g_ref[h, :, part(i)], s_ref[h]) for h in range(2))
            )
            copy = pltpu.make_async_copy(
                o_ref.at[c, part(i), :], o_out[c][i], out_sem.at[4 + 4 * c + i]
            )
            copy.start()
            stores.append(copy)
    for copy in stores:
        copy.wait()


def ffn(normed, grad, tiles):
    rows, width = normed[0].shape
    count = len(tiles)
    quarter, n3 = tiles[0][0].shape
    n = n3 // 3
    flat = [piece for pieces in tiles for piece in pieces]
    hbm = pl.BlockSpec(memory_space=pl.ANY)
    outs = pl.pallas_call(
        functools.partial(ffn_kernel, count=count),
        cost_estimate=cost(12 * rows * width * n3 * count, *flat, *flat, *normed, *grad),
        in_specs=[hbm] * (4 + 4 * count),
        out_specs=[hbm] * (4 + 4 * count),
        out_shape=[
            jax.ShapeDtypeStruct((rows, width), t) for t in (wide, narrow, wide, narrow)
        ]
        + [jax.ShapeDtypeStruct((quarter, n3), narrow)] * (4 * count),
        scratch_shapes=[
            pltpu.VMEM((2, rows, width), narrow),
            pltpu.VMEM((2, rows, width), narrow),
            pltpu.VMEM((count, width, n3), narrow),
            pltpu.VMEM((2, rows, n), narrow),
            pltpu.VMEM((2, rows, 2 * n), narrow),
            pltpu.VMEM((2, 2, rows, width), wide),
            pltpu.VMEM((2, rows, width), narrow),
            pltpu.VMEM((count, width, n3), narrow),
            pltpu.SemaphoreType.DMA((4 + 4 * count,)),
            pltpu.SemaphoreType.DMA((4 + 4 * count,)),
        ],
    )(*normed, *grad, *flat)
    return outs[:4], [outs[4 + 4 * i : 8 + 4 * i] for i in range(count)]


def ffn_cuts(total):
    cuts = []
    left = total
    while left > 0:
        take = min(tile_width, left)
        cuts.append((total - left, take))
        left -= take
    return cuts


def shards(
    size,
    tokens,
    w_query,
    w_key,
    w_value,
    w_gate,
    w_out,
    w_first,
    w_second,
    w_down,
    decay_rates,
    cotangent,
):
    send = Exchange(size)
    swap = lambda value: lax.ppermute(value, "tensor", [(0, 1), (1, 0)])
    me = lax.axis_index("dp")
    turn = lax.axis_index("tensor").astype(jnp.int32).reshape(1)
    rows, width = tokens.shape
    span = width // size
    offsets = jnp.asarray(np.repeat(block_offsets(size), span))
    place = jnp.bitwise_xor(offsets, me) * span + jnp.arange(width) % span
    shuffle = (jnp.arange(width)[:, None] == place[None, :]).astype(narrow)

    cuts = ffn_cuts(w_first.shape[1])
    down_t = w_down.T
    att = [
        Gather(send, w, i % 2 == 0)
        for i, w in enumerate((w_query, w_key, w_value, w_gate, w_out.T))
    ]
    mlp = [
        Gather(
            send,
            jnp.concatenate([w[:, at : at + n] for w in (w_first, w_second, down_t)], axis=1),
            i % 2 == 0,
        )
        for i, (at, n) in enumerate(cuts)
    ]
    bits = inner_bits(size)
    for step in range(len(att) + len(bits) + 1):
        c = step - len(bits) - 1
        if 0 <= c < len(att):
            att[c].far()
        c = step - len(bits)
        if 0 <= c < len(att):
            att[c].sides()
        for level in range(len(bits) - 1, -1, -1):
            c = step - level
            if 0 <= c < len(att):
                att[c].inner(bits[level])
            elif len(att) <= c < len(att) + len(mlp):
                mlp[c - len(att)].inner(bits[level])
    step = len(att) + len(bits) + 1
    for level in range(len(bits)):
        for c in range(max(0, step - level - len(att)), len(mlp)):
            mlp[c].inner(bits[level])
    for c in range(len(mlp) + 1):
        if c < len(mlp):
            mlp[c].sides()
        if c > 0:
            mlp[c - 1].far()
    full_q, full_k, full_v, full_u, full_o = (gather.pieces for gather in att)

    inputs = low(nn(tokens, shuffle)).astype(wide)
    scale_in = inverse_rms(inputs)
    normed_in = inputs * scale_in
    own_in = low(normed_in)
    pair_in = (own_in, swap(own_in))
    own_cot = low(nn(cotangent, shuffle))
    pair_cot = (own_cot, swap(own_cot))

    query, keys, values, slope_q, slope_k, attended, sums = front(
        turn, decay_rates, pair_in, (full_q, full_k, full_v)
    )
    proj_u = gate(pair_in, full_u)
    gated, scale_out, branch_own, branch_other = branch(
        sums, swap(sums), attended, proj_u, full_o
    )
    middle = inputs + branch_own + swap(branch_other).astype(wide)
    scale_mid = inverse_rms(middle)
    normed_mid = middle * scale_mid
    own_mid = low(normed_mid)
    pair_mid = (own_mid, swap(own_mid))

    tiles = [gather.pieces for gather in mlp]
    sums_a, grads = ffn(pair_mid, pair_cot, tiles[:-1])
    outs = [Scatter(send, grad, i % 2 == 0) for i, grad in enumerate(grads)]
    for stage in (Scatter.far, Scatter.near, Scatter.sides):
        for out in outs:
            stage(out)
    sums_b, grads = ffn(pair_mid, pair_cot, tiles[-1:])
    outs.append(Scatter(send, grads[0], len(outs) % 2 == 0))
    for stage in (Scatter.far, Scatter.near, Scatter.sides):
        stage(outs[-1])
    for out in outs:
        out.rest()

    y_sum, grad_mid_norm = (
        (sums_a[i] + sums_b[i])
        + (swap(sums_a[i + 1]).astype(wide) + swap(sums_b[i + 1]).astype(wide))
        for i in (0, 2)
    )
    grad_middle = own_cot.astype(wide) + norm_back(grad_mid_norm, normed_mid, scale_mid)
    own_e = low(grad_middle)
    pair_e = (own_e, swap(own_e))
    grad_normed, grad_unit, cross = unbranch(pair_e, attended, scale_out, proj_u, full_o)
    late = [
        Scatter(send, weight_grads(pair_e, (gated,))[0], True),
        Scatter(send, weight_grads(pair_in, (grad_unit,))[0], False),
    ]
    for stage in (Scatter.far, Scatter.near, Scatter.sides):
        for out in late:
            stage(out)
    grad_q, grad_k, grad_v = attend_back(
        turn,
        decay_rates,
        scale_out,
        cross,
        swap(cross),
        (query, keys, values, slope_q, slope_k, grad_normed, attended),
        width,
    )
    last = [
        Scatter(send, grad, i % 2 == 0)
        for i, grad in enumerate(weight_grads(pair_in, (grad_q, grad_k, grad_v)))
    ]
    for stage in (Scatter.far, Scatter.near, Scatter.sides):
        for out in last:
            stage(out)
    for out in late + last:
        out.rest()

    total_own, total_other = input_grad(
        (grad_q, grad_k, grad_v, grad_unit), (full_q, full_k, full_v, full_u)
    )
    grad_in_norm = total_own + swap(total_other).astype(wide)
    tokens_grad = grad_middle + norm_back(grad_in_norm, normed_in, scale_in)
    layer_out = low(middle + y_sum)
    layer_out = low(nt(layer_out, shuffle))
    parts = []
    rest = tokens_grad
    for _ in range(3):
        part = lax.reduce_precision(rest, 8, 7)
        parts.append(low(part))
        rest = rest - part
    tokens_grad = nt(parts[0], shuffle) + (nt(parts[1], shuffle) + nt(parts[2], shuffle))
    thirds = [
        jnp.concatenate(
            [out.total[:, i * n : (i + 1) * n] for out, (_, n) in zip(outs, cuts)], axis=1
        )
        for i in range(3)
    ]
    return (
        layer_out,
        tokens_grad,
        last[0].total,
        last[1].total,
        last[2].total,
        late[1].total,
        late[0].total.T,
        thirds[0],
        thirds[1],
        thirds[2].T,
    )


def solution(mesh):
    return jax.shard_map(
        functools.partial(shards, mesh.shape["dp"]),
        mesh=mesh,
        in_specs=(
            P(("dp", "tensor"), None),
            P("dp", "tensor"),
            P("dp", "tensor"),
            P("dp", "tensor"),
            P("dp", "tensor"),
            P("tensor", "dp"),
            P("dp", "tensor"),
            P("dp", "tensor"),
            P("tensor", "dp"),
            P("tensor"),
            P(("dp", "tensor"), None),
        ),
        out_specs=(
            P(("dp", "tensor"), None),
            P(("dp", "tensor"), None),
            P("dp", "tensor"),
            P("dp", "tensor"),
            P("dp", "tensor"),
            P("dp", "tensor"),
            P("tensor", "dp"),
            P("dp", "tensor"),
            P("dp", "tensor"),
            P("tensor", "dp"),
        ),
        check_vma=False,
    )
```

```python
import functools

import jax
import jax.numpy as jnp
import numpy as np
from jax import lax
from jax.experimental import pallas as pl
from jax.experimental.pallas import tpu as pltpu
from jax.sharding import PartitionSpec as P

eps = 1e-06
wide = jnp.float32
narrow = jnp.bfloat16
tile_width = 512


def dot(left, right, dims):
    return lax.dot_general(left, right, (dims, ((), ())), preferred_element_type=wide)


def nn(left, right):
    return dot(left, right, ((1,), (0,)))


def nt(left, right):
    return dot(left, right, ((1,), (1,)))


def tn(left, right):
    return dot(left, right, ((0,), (0,)))


def inverse_rms(values):
    return lax.rsqrt(jnp.mean(values * values, axis=-1, keepdims=True) + eps)


def norm_back(grad, normed, scale):
    return scale * (grad - normed * jnp.mean(grad * normed, axis=-1, keepdims=True))


class Exchange:

    def __init__(self, size):
        self.size = size
        self.before = {}

    def __call__(self, array, bit):
        if bit >= 4 and bit in self.before:
            (array,) = held_back((array,), self.before[bit])
        pairs = [(i, i ^ bit) for i in range(self.size)]
        result = lax.ppermute(array, "dp", pairs)
        self.before[bit] = result
        return result


def held_back(values, *waits):
    values = tuple(values)
    if not waits:
        return values
    return lax.optimization_barrier((*values, *waits))[: len(values)]


def inner_bits(size):
    bits = []
    bit = size // 2
    while bit >= 4:
        bits.append(bit)
        bit //= 2
    return bits


def block_offsets(size):
    order = [0]
    for bit in inner_bits(size) + [1, 2]:
        order = order + [entry ^ bit for entry in order]
    return np.array(order, np.int32)


class Gather:

    def __init__(self, send, shard):
        self.send = send
        self.parts = (shard,)

    def join(self, after):
        if after:
            self.parts = held_back(self.parts, *after)
        self.held = jnp.concatenate(self.parts, axis=0)

    def inner(self, level, *after):
        self.join(after)
        bit = inner_bits(self.send.size)[level]
        self.got = (self.send(self.held, bit),)
        self.parts = (self.held, *self.got)

    def rest(self, *after):
        for level in range(1, len(inner_bits(self.send.size))):
            self.inner(level, *after)

    def sides(self, *after):
        self.join(after)
        self.got = (self.send(self.held, 1), self.send(self.held, 2))

    def far(self, *after):
        half = self.held.shape[0] // 2
        side, up = held_back(self.got, *after)
        self.last = (self.send(side[:half], 2), self.send(up[half:], 1))
        self.pieces = [self.held, *self.got, *self.last]


def low(value):
    return value.astype(narrow)


def merge_kernel(up_ref, side_ref, to_up_ref, to_side_ref, up_out, side_out):
    up_out[...] = low(up_ref[...].astype(wide) + to_up_ref[...].astype(wide))
    side_out[...] = low(side_ref[...].astype(wide) + to_side_ref[...].astype(wide))


def merge(up, side, to_up, to_side):
    half = to_up.shape
    block = lambda i: pl.BlockSpec(half, lambda _: (i, 0))
    return pl.pallas_call(
        merge_kernel,
        grid=(1,),
        in_specs=[block(0), block(1), block(0), block(0)],
        out_specs=[block(0), block(1)],
        out_shape=[jax.ShapeDtypeStruct(a.shape, a.dtype) for a in (up, side)],
        input_output_aliases={0: 0, 1: 1},
        cost_estimate=cost(up.size, up, up, up),
    )(up, side, to_up, to_side)


class Scatter:

    def __init__(self, send, pieces):
        self.send = send
        self.first, self.side, self.up, *self.away = pieces
        self.moves = ["far", "sides", *reversed(inner_bits(send.size)), "end"]
        self.rest = None

    def move(self, *after):
        name = self.moves.pop(0)
        if name == "far":
            away = held_back(self.away, *after)
            self.got = tuple(self.send(a, b) for a, b in zip(away, (1, 2)))
            return
        if name == "sides":
            self.got = held_back(self.got, *after)
            self.sent = merge(self.up, self.side, *self.got)
            self.got = (self.send(self.sent[1], 1), self.send(self.sent[0], 2))
        elif name == "end":
            self.add(after)
        else:
            self.add(after)
            self.got = (self.send(self.split(), name),)

    def add(self, after):
        got = held_back(self.got, *after)
        rest = self.first.astype(wide) if self.rest is None else self.rest
        self.total = rest + sum(g.astype(wide) for g in got)

    def split(self):
        half = self.total.shape[0] // 2
        self.rest = self.total[:half]
        return low(self.total[half:])


def move_along(scatters, *after):
    name = scatters[0].moves[0]
    assert all(out.moves[0] == name for out in scatters)
    parts = []
    for out in scatters:
        out.moves.pop(0)
        out.add(after)
        parts.append(out.split())
    got = scatters[0].send(jnp.concatenate(parts, axis=1), name)
    at = 0
    for out, part in zip(scatters, parts):
        out.got = (got[:, at : at + part.shape[1]],)
        at += part.shape[1]


def tables(rate, size):
    row = lax.broadcasted_iota(jnp.int32, (size, 1), 0).astype(wide)
    col = lax.broadcasted_iota(jnp.int32, (1, size), 1).astype(wide)
    ahead = jnp.exp(-rate * row)
    inner = jnp.where(col <= row, ahead * jnp.exp(rate * col), 0.0)
    outof = jnp.exp(-rate * (size - row))
    return inner, ahead, outof


def cost(flops, *arrays):
    size = sum(a.size * jnp.dtype(a.dtype).itemsize for a in arrays)
    return pl.CostEstimate(flops=int(flops), transcendentals=0, bytes_accessed=int(size))


def rows_of(refs):
    half = refs[0].shape[0]
    return [(ref, slice(i * half, (i + 1) * half)) for i, ref in enumerate(refs)]


def join(refs):
    return jnp.concatenate([ref[...] for ref in refs], axis=0)


def row_sums(values):
    ones = jnp.ones((8, values.shape[1]), wide)
    return lax.dot_general(
        ones,
        values,
        (((1,), (1,)), ((), ())),
        precision=lax.Precision.HIGHEST,
        preferred_element_type=wide,
    )


def column(own, other):
    half = own.shape[1] // 2
    total = own + jnp.concatenate([other[:, half:], other[:, :half]], axis=1)
    return jnp.transpose(total)[:, :1]


def spans(turn_ref, size):
    turn = turn_ref[0]
    early = pl.ds(pl.multiple_of(turn * size, size), size)
    late = pl.ds(pl.multiple_of((1 - turn) * size, size), size)
    return early, late


def cumulative(refs):
    at = 0
    result = []
    for ref in refs:
        result.append((ref, slice(at, at + ref.shape[0])))
        at += ref.shape[0]
    return result


def whole(array):
    return pl.BlockSpec(array.shape, lambda i: (0, 0))


def columns_of(pieces, j, width):
    return [pl.BlockSpec((p.shape[0], width), lambda i: (0, j)) for p in pieces]


def front_kernel(turn_ref, rate_ref, own_ref, other_ref, *refs, heads):
    wq, wk, wv = refs[0:5], refs[5:10], refs[10:15]
    q_ref, k_ref, v_ref, sq_ref, sk_ref, o_ref, sum_ref = refs[15:]
    pair = rows_of((own_ref, other_ref))
    for pieces, out, slope in ((wq, q_ref, sq_ref), (wk, k_ref, sk_ref)):
        weight = join(pieces)
        for ref, rows in pair:
            value = nn(ref[...], weight)
            sigma = jax.nn.sigmoid(value)
            out[rows, :] = low(value * sigma)
            slope[rows, :] = low(sigma * (1.0 + value * (1.0 - sigma)))
    weight = join(wv)
    for ref, rows in pair:
        v_ref[rows, :] = low(nn(ref[...], weight))
    size = own_ref.shape[0]
    early, late = spans(turn_ref, size)
    wide_head = q_ref.shape[1] // heads
    sums = 0.0
    for j in range(heads):
        cols = slice(j * wide_head, (j + 1) * wide_head)
        inner, ahead, outof = tables(rate_ref[pl.program_id(0) * heads + j], size)

        def local(rows):
            weights = low(nt(q_ref[rows, cols], k_ref[rows, cols]) * inner)
            return nn(weights, v_ref[rows, cols])

        weighted = low(k_ref[early, cols].astype(wide) * outof)
        state = low(tn(weighted, v_ref[early, cols]))
        o_ref[early, cols] = local(early)
        o_ref[late, cols] = local(late) + nn(q_ref[late, cols], state) * ahead
    values = o_ref[...]
    sums = row_sums(values * values)

    @pl.when(pl.program_id(0) == 0)
    def _():
        sum_ref[...] = sums

    @pl.when(pl.program_id(0) > 0)
    def _():
        sum_ref[...] += sums


def front(turn, rates, pair, pieces):
    rows, width = pair[0].shape
    columns = pieces[0].shape[1] // 3
    steps = 2
    block = columns // steps
    scalar = pl.BlockSpec(memory_space=pltpu.SMEM)
    piece = lambda p, j: pl.BlockSpec((p.shape[0], block), lambda i: (0, i + steps * j))
    out = pl.BlockSpec((2 * rows, block), lambda i: (0, i))
    sums = jax.ShapeDtypeStruct((8, 2 * rows), wide)
    types = [narrow] * 5 + [wide]
    return pl.pallas_call(
        functools.partial(front_kernel, heads=rates.shape[0] // steps),
        cost_estimate=cost(18 * rows * width * columns, *pair, *pair, *pair, *pair, *pair),
        grid=(steps,),
        in_specs=[scalar, scalar]
        + [whole(p) for p in pair]
        + [piece(p, j) for j in range(3) for p in pieces],
        out_specs=[out] * 6 + [whole(sums)],
        out_shape=[jax.ShapeDtypeStruct((2 * rows, columns), t) for t in types] + [sums],
    )(turn, rates, *pair, *pieces, *pieces, *pieces)


def gate_kernel(own_ref, other_ref, *refs):
    weight = join(refs[:-1])
    for ref, rows in rows_of((own_ref, other_ref)):
        refs[-1][rows, :] = nn(ref[...], weight).astype(refs[-1].dtype)


def gate(pair, pieces):
    rows, width = pair[0].shape
    columns = pieces[0].shape[1] // 2
    out = jax.ShapeDtypeStruct((2 * rows, columns), wide)
    return pl.pallas_call(
        gate_kernel,
        cost_estimate=cost(4 * rows * width * columns, *pair, *pair),
        grid=(1,),
        in_specs=[whole(p) for p in pair] + columns_of(pieces, 0, columns),
        out_specs=whole(out),
        out_shape=out,
    )(*pair, *pieces)


def branch_kernel(sum_ref, got_ref, o_ref, u_ref, *refs):
    pieces, (gated_ref, scale_ref, own_ref, other_ref) = refs[:5], refs[5:]
    rows, width = own_ref.shape
    scale = lax.rsqrt(column(sum_ref[...], got_ref[...]) / width + eps)
    scale_ref[...] = scale
    gated_ref[...] = low(o_ref[...] * scale * u_ref[...])
    for ref, cols in cumulative(pieces):
        value = nt(gated_ref[...], ref[...])
        own_ref[:, cols] = value[:rows]
        other_ref[:, cols] = low(value[rows:])


def branch(sums, got, attended, proj_u, pieces):
    length, columns = attended.shape
    rows, width = length // 2, sum(p.shape[0] for p in pieces)
    ins = (sums, got, attended, proj_u)
    outs = [
        jax.ShapeDtypeStruct((length, columns), narrow),
        jax.ShapeDtypeStruct((length, 1), wide),
        jax.ShapeDtypeStruct((rows, width), wide),
        jax.ShapeDtypeStruct((rows, width), narrow),
    ]
    return pl.pallas_call(
        branch_kernel,
        cost_estimate=cost(2 * length * columns * width, attended, attended, attended, proj_u),
        grid=(1,),
        in_specs=[whole(a) for a in ins] + columns_of(pieces, 1, columns),
        out_specs=[whole(a) for a in outs],
        out_shape=outs,
    )(*ins, *pieces)


def unbranch_kernel(own_ref, other_ref, o_ref, scale_ref, u_ref, *refs):
    pieces, (grad_ref, unit_ref, cross_ref) = refs[:5], refs[5:]
    weight = join(pieces)
    for ref, rows in rows_of((own_ref, other_ref)):
        value = nn(ref[...], weight)
        normed = o_ref[rows, :] * scale_ref[rows, :]
        unit_ref[rows, :] = low(value * normed)
        value = value * u_ref[rows, :]
        grad_ref[rows, :] = value
        cross_ref[:, rows] = row_sums(value * normed)


def unbranch(pair, attended, scale, proj_u, pieces):
    length, columns = attended.shape
    width = pair[0].shape[1]
    ins = (*pair, attended, scale, proj_u)
    outs = [
        jax.ShapeDtypeStruct((length, columns), wide),
        jax.ShapeDtypeStruct((length, columns), narrow),
        jax.ShapeDtypeStruct((8, length), wide),
    ]
    return pl.pallas_call(
        unbranch_kernel,
        cost_estimate=cost(2 * length * columns * width, attended, attended, attended, proj_u),
        grid=(1,),
        in_specs=[whole(a) for a in ins] + columns_of(pieces, 1, columns),
        out_specs=[whole(a) for a in outs],
        out_shape=outs,
    )(*ins, *pieces)


def attend_back_kernel(
    turn_ref,
    rate_ref,
    scale_ref,
    cross_ref,
    got_ref,
    q_ref,
    k_ref,
    v_ref,
    sq_ref,
    sk_ref,
    gn_ref,
    o_ref,
    dq_ref,
    dk_ref,
    dv_ref,
    g_ref,
    c_ref,
    *,
    width,
):
    size = q_ref.shape[0] // 2
    inner, ahead, outof = tables(rate_ref[pl.program_id(0)], size)
    early, late = spans(turn_ref, size)

    @pl.when(pl.program_id(0) == 0)
    def _():
        c_ref[...] = column(cross_ref[...], got_ref[...]) / width

    scale = scale_ref[...]
    normed = o_ref[...] * scale
    g_ref[...] = low(scale * (gn_ref[...] - normed * c_ref[...]))

    def local(rows):
        q, k, v, g = (ref[rows, :] for ref in (q_ref, k_ref, v_ref, g_ref))
        weights = low(nt(q, k) * inner)
        grad_scores = low(nt(g, v) * inner)
        return nn(grad_scores, k), tn(grad_scores, q), tn(weights, g)

    def store(rows, dq, dk, dv):
        dq_ref[rows, :] = low(dq * sq_ref[rows, :].astype(wide))
        dk_ref[rows, :] = low(dk * sk_ref[rows, :].astype(wide))
        dv_ref[rows, :] = low(dv)

    weighted = low(k_ref[early, :].astype(wide) * outof)
    state = low(tn(weighted, v_ref[early, :]))
    g_ahead = low(g_ref[late, :].astype(wide) * ahead)
    grad_state = low(tn(q_ref[late, :], g_ahead))
    dq, dk, dv = local(late)
    store(late, dq + nt(g_ahead, state), dk, dv)
    dq, dk, dv = local(early)
    store(
        early,
        dq,
        dk + nt(v_ref[early, :], grad_state) * outof,
        dv + nn(weighted, grad_state),
    )


def attend_back(turn, rates, scale, cross, got, arrays, width):
    heads = rates.shape[0]
    length, columns = arrays[0].shape
    spec = pl.BlockSpec((length, columns // heads), lambda h: (0, h))
    col = pl.BlockSpec((length, 1), lambda h: (0, 0))
    row = pl.BlockSpec((8, length), lambda h: (0, 0))
    scalar = pl.BlockSpec(memory_space=pltpu.SMEM)
    return pl.pallas_call(
        functools.partial(attend_back_kernel, width=width),
        cost_estimate=cost(12 * length * length * columns, *arrays, *arrays, *arrays),
        grid=(heads,),
        in_specs=[scalar, scalar, col, row, row] + [spec] * len(arrays),
        out_specs=[spec] * 3,
        out_shape=[jax.ShapeDtypeStruct((length, columns), narrow)] * 3,
        scratch_shapes=[
            pltpu.VMEM((length, columns // heads), narrow),
            pltpu.VMEM((length, 1), wide),
        ],
    )(turn, rates, scale, cross, got, *arrays)


def weight_grad_kernel(*refs, count, each):
    pairs, refs = [refs[2 * j : 2 * j + 2] for j in range(each)], refs[2 * each :]
    arrays, outs = refs[:count], refs[count:]
    columns = arrays[0].shape[1]
    for out, cols in cumulative(outs):
        for j, array in enumerate(arrays):
            pair = rows_of(pairs[j % each])
            total = sum(tn(ref[:, cols], array[rows, :]) for ref, rows in pair)
            out[:, j * columns : (j + 1) * columns] = low(total)


def piece_rows(width):
    return [width // 4] * 3 + [width // 8] * 2


def weight_grads(pairs, arrays):
    rows, width = pairs[0][0].shape
    columns = arrays[0].shape[1]
    count = len(arrays)
    return pl.pallas_call(
        functools.partial(weight_grad_kernel, count=count, each=len(pairs)),
        cost_estimate=cost(4 * rows * width * columns * count, *pairs[0], *arrays, *arrays),
        out_shape=[
            jax.ShapeDtypeStruct((r, count * columns), narrow) for r in piece_rows(width)
        ],
    )(*(a for pair in pairs for a in pair), *arrays)


def input_grad_kernel(*refs):
    grads, refs, (own_ref, other_ref) = refs[:4], refs[4:24], refs[24:]
    pieces = [cumulative(refs[5 * j : 5 * j + 5]) for j in range(4)]
    rows = own_ref.shape[0]
    for i in range(5):
        cols = pieces[0][i][1]
        value = sum(nt(grads[j][...], pieces[j][i][0][...]) for j in range(4))
        own_ref[:, cols] = value[:rows]
        other_ref[:, cols] = low(value[rows:])


def input_grad(grads, first, second):
    length, columns = grads[0].shape
    rows, width = length // 2, sum(p.shape[0] for p in first)
    outs = [
        jax.ShapeDtypeStruct((rows, width), wide),
        jax.ShapeDtypeStruct((rows, width), narrow),
    ]
    return pl.pallas_call(
        input_grad_kernel,
        cost_estimate=cost(8 * length * columns * width, *grads, *grads, *grads),
        grid=(1,),
        in_specs=[whole(g) for g in grads]
        + [spec for j in range(3) for spec in columns_of(first, j, columns)]
        + columns_of(second, 0, columns),
        out_specs=[whole(a) for a in outs],
        out_shape=outs,
    )(*grads, *first, *first, *first, *second)


def ffn_kernel(*refs, chained, last):
    n_in, g_in, w_in = refs[0:2], refs[2:4], refs[4:9]
    refs = refs[9:]
    if chained:
        before, refs = refs[:4], refs[4:]
    sums_out, o_out = refs[0:4], refs[4:9]
    n_ref, g_ref, w_ref, s_ref, d_ref, acc_ref, low_ref, o_ref, in_sem, out_sem = refs[9:]
    rows = n_ref.shape[1]
    n = s_ref.shape[2]
    pieces = cumulative(w_in)

    load = [
        pltpu.make_async_copy(ref, w_ref.at[part, :], in_sem.at[4 + i])
        for i, (ref, part) in enumerate(pieces)
    ]
    load += [pltpu.make_async_copy(n_in[h], n_ref.at[h], in_sem.at[h]) for h in range(2)]
    load += [pltpu.make_async_copy(g_in[h], g_ref.at[h], in_sem.at[2 + h]) for h in range(2)]
    for copy in load:
        copy.start()
    accs = [acc_ref.at[k // 2, k % 2] for k in range(4)]
    fill = []
    if chained:
        fill = [pltpu.make_async_copy(before[k], accs[k], in_sem.at[9 + k]) for k in range(4)]
    for copy in fill:
        copy.start()
    for copy in load:
        copy.wait()

    def half(h, carry):
        ab = nn(n_ref[h], w_ref[:, : 2 * n])
        ds = nn(g_ref[h], w_ref[:, 2 * n :])
        a = ab[:, :n]
        b = ab[:, n:]
        s_ref[h] = low(a * b)
        d_ref[h, :, :n] = low(ds * b)
        d_ref[h, :, n:] = low(ds * a)
        return carry

    lax.fori_loop(0, 2, half, 0)
    for copy in fill:
        copy.wait()
    y = nt(s_ref[...].reshape(2 * rows, n), w_ref[:, 2 * n :]).reshape(2, rows, -1)
    d = nt(d_ref[...].reshape(2 * rows, 2 * n), w_ref[:, : 2 * n]).reshape(2, rows, -1)
    for k, value in enumerate((y, d)):
        if chained:
            acc_ref[k] += value
        else:
            acc_ref[k] = value
    stores = []
    for k in range(4):
        source = accs[k]
        if last and k % 2 == 1:
            low_ref[k // 2] = low(acc_ref[k // 2, 1])
            source = low_ref.at[k // 2]
        stores.append(pltpu.make_async_copy(source, sums_out[k], out_sem.at[k]))
        stores[-1].start()
    for i, (_, part) in reversed(list(enumerate(pieces))):
        o_ref[part, : 2 * n] = low(sum(tn(n_ref[h, :, part], d_ref[h]) for h in range(2)))
        o_ref[part, 2 * n :] = low(sum(tn(g_ref[h, :, part], s_ref[h]) for h in range(2)))
        stores.append(pltpu.make_async_copy(o_ref.at[part, :], o_out[i], out_sem.at[4 + i]))
        stores[-1].start()
    for copy in stores:
        copy.wait()


def ffn(normed, grad, pieces, sums, last):
    rows, width = normed[0].shape
    n3 = pieces[0].shape[1]
    n = n3 // 3
    hbm = pl.BlockSpec(memory_space=pl.ANY)
    ins = (*normed, *grad, *pieces, *(sums or ()))
    other = narrow if last else wide
    outs = pl.pallas_call(
        functools.partial(ffn_kernel, chained=sums is not None, last=last),
        cost_estimate=cost(12 * rows * width * n3, *ins, *ins),
        in_specs=[hbm] * len(ins),
        out_specs=[hbm] * 9,
        out_shape=[jax.ShapeDtypeStruct((rows, width), t) for t in (wide, other, wide, other)]
        + [jax.ShapeDtypeStruct((r, n3), narrow) for r in piece_rows(width)],
        scratch_shapes=[
            pltpu.VMEM((2, rows, width), narrow),
            pltpu.VMEM((2, rows, width), narrow),
            pltpu.VMEM((width, n3), narrow),
            pltpu.VMEM((2, rows, n), narrow),
            pltpu.VMEM((2, rows, 2 * n), narrow),
            pltpu.VMEM((2, 2, rows, width), wide),
            pltpu.VMEM((2, rows, width), narrow),
            pltpu.VMEM((width, n3), narrow),
            pltpu.SemaphoreType.DMA((13,)),
            pltpu.SemaphoreType.DMA((9,)),
        ],
    )(*ins)
    return outs[:4], outs[4:]


def ffn_cuts(total):
    cuts = []
    left = total
    while left > 0:
        take = min(tile_width, left)
        cuts.append((total - left, take))
        left -= take
    return cuts


def shards(
    size,
    tokens,
    w_query,
    w_key,
    w_value,
    w_gate,
    w_out,
    w_first,
    w_second,
    w_down,
    decay_rates,
    cotangent,
):
    send = Exchange(size)
    swap = lambda value: lax.ppermute(value, "tensor", [(0, 1), (1, 0)])
    me = lax.axis_index("dp")
    turn = lax.axis_index("tensor").astype(jnp.int32).reshape(1)
    rows, width = tokens.shape
    span = width // size
    offsets = jnp.asarray(np.repeat(block_offsets(size), span))
    place = jnp.bitwise_xor(offsets, me) * span + jnp.arange(width) % span
    shuffle = (jnp.arange(width)[:, None] == place[None, :]).astype(narrow)

    cuts = ffn_cuts(w_first.shape[1])
    down_t = w_down.T
    beside = lambda *arrays: jnp.concatenate(arrays, axis=1)
    first = Gather(send, beside(w_query, w_key, w_value))
    second = Gather(send, beside(w_gate, w_out.T))
    mlp = [
        Gather(send, beside(*(w[:, at : at + n] for w in (w_first, w_second, down_t))))
        for at, n in cuts
    ]
    first.inner(0)
    first.rest()
    second.inner(0, *first.parts[1:])
    first.sides()
    second.rest()
    first.far()
    second.sides(*first.got)
    mlp[0].inner(0, *first.got)

    inputs = low(nn(tokens, shuffle)).astype(wide)
    scale_in = inverse_rms(inputs)
    normed_in = inputs * scale_in
    own_in = low(normed_in)
    pair_in = (own_in, swap(own_in))
    own_cot = low(nn(cotangent, shuffle))
    pair_cot = (own_cot, swap(own_cot))

    pair_in = held_back(pair_in, pair_cot[1])
    query, keys, values, slope_q, slope_k, attended, sums = front(
        turn, decay_rates, pair_in, first.pieces
    )
    attended, sums = held_back((attended, sums), *second.got)
    second.far(attended)
    mlp[0].rest(attended)
    pair_gate = held_back(pair_in, attended)
    mlp[0].sides(*second.last)
    mlp[1].inner(0, attended)
    mlp[1].rest(*second.last)
    mlp[2].inner(0, *second.last)
    proj_u = gate(pair_gate, second.pieces)
    (attended_late,) = held_back((attended,), proj_u)
    gated, scale_out, branch_own, branch_other = branch(
        sums, swap(sums), attended_late, proj_u, second.pieces
    )
    branch_own, branch_other, gated = held_back(
        (branch_own, branch_other, gated), *mlp[0].got, *mlp[1].got, *mlp[2].got
    )
    mlp[0].far(gated)
    mlp[2].rest(gated)
    middle = inputs + branch_own + swap(branch_other).astype(wide)
    scale_mid = inverse_rms(middle)
    normed_mid = middle * scale_mid
    own_mid = low(normed_mid)
    mlp[1].sides(*mlp[0].last)
    mlp[2].sides(*mlp[0].last)
    pair_mid = (own_mid, swap(own_mid))

    pair_mid = held_back(pair_mid, *mlp[2].parts)
    sums, grads = ffn(pair_mid, pair_cot, mlp[0].pieces, None, False)
    outs = [Scatter(send, grads)]
    mlp[1].far(grads[0])
    mlp[2].far(grads[0])
    outs[0].move(grads[0])
    sums, grads = ffn(pair_mid, pair_cot, mlp[1].pieces, sums, False)
    grads = held_back(grads, *mlp[2].last, *outs[0].got)
    outs.append(Scatter(send, grads))
    outs[1].move(grads[0])
    outs[0].move(grads[0])
    pair_mid = held_back(pair_mid, *outs[0].sent)
    sums, grads = ffn(pair_mid, pair_cot, mlp[2].pieces, sums, True)
    outs.append(Scatter(send, grads))
    y_own, y_other, d_own, d_other = held_back(sums, *outs[1].got)
    outs[2].move(d_other)

    grad_mid_norm = d_own + swap(d_other).astype(wide)
    grad_middle = own_cot.astype(wide) + norm_back(grad_mid_norm, normed_mid, scale_mid)
    own_e = low(grad_middle)
    pair_e = (own_e, swap(own_e))
    outs[1].move(own_e)
    pair_e_late = held_back(pair_e, *outs[1].sent, *outs[0].got)
    grad_normed, grad_unit, cross = unbranch(pair_e_late, attended, scale_out, proj_u, second.pieces)
    other_cross = swap(cross)
    pair_in_late = held_back(pair_in, grad_unit)
    grads = weight_grads((pair_in_late, pair_e), (grad_unit, gated))
    late = Scatter(send, grads)
    outs[0].move(grads[0], other_cross)
    (grad_normed,) = held_back((grad_normed,), grads[0])
    outs[2].move(grads[0])
    grad_q, grad_k, grad_v = held_back(
        attend_back(
            turn,
            decay_rates,
            scale_out,
            cross,
            other_cross,
            (query, keys, values, slope_q, slope_k, grad_normed, attended),
            width,
        ),
        *outs[0].got,
    )
    grads = weight_grads((pair_in,), (grad_q, grad_k, grad_v))
    last = Scatter(send, grads)
    (grad_q_late,) = held_back((grad_q,), grads[0], *outs[1].got, *outs[2].got)
    move_along(outs[1:], grads[0])
    last.move(grads[0])
    late.move(grads[0])
    total_own, total_other = held_back(
        input_grad((grad_q_late, grad_k, grad_v, grad_unit), first.pieces, second.pieces),
        *last.got,
        *late.got,
    )
    last.move(total_own)
    late.move(total_own, *last.sent)
    while len(outs[0].moves) > 1:
        move_along(outs, total_own, *late.sent)
    last.move(*outs[2].got)
    late.move(*last.sent, *outs[2].got)
    (y_other,) = held_back((y_other,), *outs[2].got)
    for out in (*outs, last, late):
        while out.moves:
            out.move(total_own)
    grad_in_norm = total_own + swap(total_other).astype(wide)
    tokens_grad = grad_middle + norm_back(grad_in_norm, normed_in, scale_in)
    y_sum = y_own + swap(y_other).astype(wide)
    layer_out = low(middle + y_sum)
    layer_out = low(nt(layer_out, shuffle))
    parts = []
    rest = tokens_grad
    for _ in range(3):
        part = lax.reduce_precision(rest, 8, 7)
        parts.append(low(part))
        rest = rest - part
    tokens_grad = nt(parts[0], shuffle) + (nt(parts[1], shuffle) + nt(parts[2], shuffle))
    thirds = [
        jnp.concatenate(
            [out.total[:, i * n : (i + 1) * n] for out, (_, n) in zip(outs, cuts)], axis=1
        )
        for i in range(3)
    ]
    n = w_query.shape[1]
    return (
        layer_out,
        tokens_grad,
        last.total[:, :n],
        last.total[:, n : 2 * n],
        last.total[:, 2 * n :],
        late.total[:, :n],
        late.total[:, n:].T,
        thirds[0],
        thirds[1],
        thirds[2].T,
    )


def solution(mesh):
    return jax.shard_map(
        functools.partial(shards, mesh.shape["dp"]),
        mesh=mesh,
        in_specs=(
            P(("dp", "tensor"), None),
            P("dp", "tensor"),
            P("dp", "tensor"),
            P("dp", "tensor"),
            P("dp", "tensor"),
            P("tensor", "dp"),
            P("dp", "tensor"),
            P("dp", "tensor"),
            P("tensor", "dp"),
            P("tensor"),
            P(("dp", "tensor"), None),
        ),
        out_specs=(
            P(("dp", "tensor"), None),
            P(("dp", "tensor"), None),
            P("dp", "tensor"),
            P("dp", "tensor"),
            P("dp", "tensor"),
            P("dp", "tensor"),
            P("tensor", "dp"),
            P("dp", "tensor"),
            P("dp", "tensor"),
            P("tensor", "dp"),
        ),
        check_vma=False,
    )
```

```python
import functools

import jax
import jax.numpy as jnp
import numpy as np
from jax import lax
from jax.experimental import pallas as pl
from jax.experimental.pallas import tpu as pltpu
from jax.sharding import PartitionSpec as P

eps = 1e-06
wide = jnp.float32
narrow = jnp.bfloat16
tile_width = 512


def dot(left, right, dims):
    return lax.dot_general(left, right, (dims, ((), ())), preferred_element_type=wide)


def nn(left, right):
    return dot(left, right, ((1,), (0,)))


def nt(left, right):
    return dot(left, right, ((1,), (1,)))


def tn(left, right):
    return dot(left, right, ((0,), (0,)))


def inverse_rms(values):
    return lax.rsqrt(jnp.mean(values * values, axis=-1, keepdims=True) + eps)


def norm_back(grad, normed, scale):
    return scale * (grad - normed * jnp.mean(grad * normed, axis=-1, keepdims=True))


class Exchange:

    def __init__(self, size):
        self.size = size
        self.before = {}

    def __call__(self, array, bit):
        if bit >= 4 and bit in self.before:
            (array,) = held_back((array,), self.before[bit])
        pairs = [(i, i ^ bit) for i in range(self.size)]
        result = lax.ppermute(array, "dp", pairs)
        self.before[bit] = result
        return result


def held_back(values, *waits):
    values = tuple(values)
    if not waits:
        return values
    return lax.optimization_barrier((*values, *waits))[: len(values)]


def inner_bits(size):
    bits = []
    bit = size // 2
    while bit >= 4:
        bits.append(bit)
        bit //= 2
    return bits


def block_offsets(size):
    order = [0]
    for bit in inner_bits(size) + [1, 2]:
        order = order + [entry ^ bit for entry in order]
    return np.array(order, np.int32)


class Gather:

    def __init__(self, send, shard):
        self.send = send
        self.parts = (shard,)

    def join(self, after):
        if after:
            self.parts = held_back(self.parts, *after)
        self.held = jnp.concatenate(self.parts, axis=0)

    def inner(self, level, *after):
        self.join(after)
        bit = inner_bits(self.send.size)[level]
        self.got = (self.send(self.held, bit),)
        self.parts = (self.held, *self.got)

    def rest(self, *after):
        for level in range(1, len(inner_bits(self.send.size))):
            self.inner(level, *after)

    def sides(self, *after):
        self.join(after)
        self.got = (self.send(self.held, 1), self.send(self.held, 2))

    def far(self, *after):
        half = self.held.shape[0] // 2
        side, up = held_back(self.got, *after)
        self.last = (self.send(side[:half], 2), self.send(up[half:], 1))
        self.pieces = [self.held, *self.got, *self.last]


def low(value):
    return value.astype(narrow)


def merge_kernel(up_ref, side_ref, to_up_ref, to_side_ref, up_out, side_out):
    up_out[...] = low(up_ref[...].astype(wide) + to_up_ref[...].astype(wide))
    side_out[...] = low(side_ref[...].astype(wide) + to_side_ref[...].astype(wide))


def merge(up, side, to_up, to_side):
    half = to_up.shape
    block = lambda i: pl.BlockSpec(half, lambda _: (i, 0))
    return pl.pallas_call(
        merge_kernel,
        grid=(1,),
        in_specs=[block(0), block(1), block(0), block(0)],
        out_specs=[block(0), block(1)],
        out_shape=[jax.ShapeDtypeStruct(a.shape, a.dtype) for a in (up, side)],
        input_output_aliases={0: 0, 1: 1},
        cost_estimate=cost(up.size, up, up, up),
    )(up, side, to_up, to_side)


class Scatter:

    def __init__(self, send, pieces):
        self.send = send
        self.first, self.side, self.up, *self.away = pieces
        self.moves = ["far", "sides", *reversed(inner_bits(send.size)), "end"]
        self.rest = None

    def move(self, *after):
        name = self.moves.pop(0)
        if name == "far":
            away = held_back(self.away, *after)
            self.got = tuple(self.send(a, b) for a, b in zip(away, (1, 2)))
            return
        if name == "sides":
            self.got = held_back(self.got, *after)
            self.sent = merge(self.up, self.side, *self.got)
            self.got = (self.send(self.sent[1], 1), self.send(self.sent[0], 2))
        elif name == "end":
            self.add(after)
        else:
            self.add(after)
            self.got = (self.send(self.split(), name),)

    def add(self, after):
        got = held_back(self.got, *after)
        rest = self.first.astype(wide) if self.rest is None else self.rest
        self.total = rest + sum(g.astype(wide) for g in got)

    def split(self):
        half = self.total.shape[0] // 2
        self.rest = self.total[:half]
        return low(self.total[half:])


def move_along(scatters, *after):
    name = scatters[0].moves[0]
    assert all(out.moves[0] == name for out in scatters)
    parts = []
    for out in scatters:
        out.moves.pop(0)
        out.add(after)
        parts.append(out.split())
    got = scatters[0].send(jnp.concatenate(parts, axis=1), name)
    at = 0
    for out, part in zip(scatters, parts):
        out.got = (got[:, at : at + part.shape[1]],)
        at += part.shape[1]


def tables(rate, size):
    row = lax.broadcasted_iota(jnp.int32, (size, 1), 0).astype(wide)
    col = lax.broadcasted_iota(jnp.int32, (1, size), 1).astype(wide)
    ahead = jnp.exp(-rate * row)
    inner = jnp.where(col <= row, ahead * jnp.exp(rate * col), 0.0)
    outof = jnp.exp(-rate * (size - row))
    return inner, ahead, outof


def cost(flops, *arrays):
    size = sum(a.size * jnp.dtype(a.dtype).itemsize for a in arrays)
    return pl.CostEstimate(flops=int(flops), transcendentals=0, bytes_accessed=int(size))


def rows_of(refs):
    half = refs[0].shape[0]
    return [(ref, slice(i * half, (i + 1) * half)) for i, ref in enumerate(refs)]


def join(refs):
    return jnp.concatenate([ref[...] for ref in refs], axis=0)


def row_sums(values):
    ones = jnp.ones((8, values.shape[1]), wide)
    return lax.dot_general(
        ones,
        values,
        (((1,), (1,)), ((), ())),
        precision=lax.Precision.HIGHEST,
        preferred_element_type=wide,
    )


def column(own, other):
    half = own.shape[1] // 2
    total = own + jnp.concatenate([other[:, half:], other[:, :half]], axis=1)
    return jnp.transpose(total)[:, :1]


def spans(turn_ref, size):
    turn = turn_ref[0]
    early = pl.ds(pl.multiple_of(turn * size, size), size)
    late = pl.ds(pl.multiple_of((1 - turn) * size, size), size)
    return early, late


def cumulative(refs):
    at = 0
    result = []
    for ref in refs:
        result.append((ref, slice(at, at + ref.shape[0])))
        at += ref.shape[0]
    return result


def whole(array):
    return pl.BlockSpec(array.shape, lambda i: (0, 0))


def columns_of(pieces, j, width):
    return [pl.BlockSpec((p.shape[0], width), lambda i: (0, j)) for p in pieces]


def front_kernel(turn_ref, rate_ref, own_ref, other_ref, *refs, heads):
    wq, wk, wv = refs[0:5], refs[5:10], refs[10:15]
    q_ref, k_ref, v_ref, sq_ref, sk_ref, o_ref, sum_ref = refs[15:]
    pair = rows_of((own_ref, other_ref))
    for pieces, out, slope in ((wq, q_ref, sq_ref), (wk, k_ref, sk_ref)):
        weight = join(pieces)
        for ref, rows in pair:
            value = nn(ref[...], weight)
            sigma = jax.nn.sigmoid(value)
            out[rows, :] = low(value * sigma)
            slope[rows, :] = low(sigma * (1.0 + value * (1.0 - sigma)))
    weight = join(wv)
    for ref, rows in pair:
        v_ref[rows, :] = low(nn(ref[...], weight))
    size = own_ref.shape[0]
    early, late = spans(turn_ref, size)
    wide_head = q_ref.shape[1] // heads
    sums = 0.0
    for j in range(heads):
        cols = slice(j * wide_head, (j + 1) * wide_head)
        inner, ahead, outof = tables(rate_ref[pl.program_id(0) * heads + j], size)

        def local(rows):
            weights = low(nt(q_ref[rows, cols], k_ref[rows, cols]) * inner)
            return nn(weights, v_ref[rows, cols])

        weighted = low(k_ref[early, cols].astype(wide) * outof)
        state = low(tn(weighted, v_ref[early, cols]))
        o_ref[early, cols] = local(early)
        o_ref[late, cols] = local(late) + nn(q_ref[late, cols], state) * ahead
    values = o_ref[...]
    sums = row_sums(values * values)

    @pl.when(pl.program_id(0) == 0)
    def _():
        sum_ref[...] = sums

    @pl.when(pl.program_id(0) > 0)
    def _():
        sum_ref[...] += sums


def front(turn, rates, pair, pieces):
    rows, width = pair[0].shape
    columns = pieces[0].shape[1] // 3
    steps = 2
    block = columns // steps
    scalar = pl.BlockSpec(memory_space=pltpu.SMEM)
    piece = lambda p, j: pl.BlockSpec((p.shape[0], block), lambda i: (0, i + steps * j))
    out = pl.BlockSpec((2 * rows, block), lambda i: (0, i))
    sums = jax.ShapeDtypeStruct((8, 2 * rows), wide)
    types = [narrow] * 5 + [wide]
    return pl.pallas_call(
        functools.partial(front_kernel, heads=rates.shape[0] // steps),
        cost_estimate=cost(18 * rows * width * columns, *pair, *pair, *pair, *pair, *pair),
        grid=(steps,),
        in_specs=[scalar, scalar]
        + [whole(p) for p in pair]
        + [piece(p, j) for j in range(3) for p in pieces],
        out_specs=[out] * 6 + [whole(sums)],
        out_shape=[jax.ShapeDtypeStruct((2 * rows, columns), t) for t in types] + [sums],
    )(turn, rates, *pair, *pieces, *pieces, *pieces)


def gate_kernel(own_ref, other_ref, *refs):
    weight = join(refs[:-1])
    for ref, rows in rows_of((own_ref, other_ref)):
        refs[-1][rows, :] = nn(ref[...], weight).astype(refs[-1].dtype)


def gate(pair, pieces):
    rows, width = pair[0].shape
    columns = pieces[0].shape[1] // 2
    out = jax.ShapeDtypeStruct((2 * rows, columns), wide)
    return pl.pallas_call(
        gate_kernel,
        cost_estimate=cost(4 * rows * width * columns, *pair, *pair),
        grid=(1,),
        in_specs=[whole(p) for p in pair] + columns_of(pieces, 0, columns),
        out_specs=whole(out),
        out_shape=out,
    )(*pair, *pieces)


def branch_kernel(sum_ref, got_ref, o_ref, u_ref, *refs):
    pieces, (gated_ref, scale_ref, own_ref, other_ref) = refs[:5], refs[5:]
    rows, width = own_ref.shape
    scale = lax.rsqrt(column(sum_ref[...], got_ref[...]) / width + eps)
    scale_ref[...] = scale
    gated_ref[...] = low(o_ref[...] * scale * u_ref[...])
    for ref, cols in cumulative(pieces):
        value = nt(gated_ref[...], ref[...])
        own_ref[:, cols] = value[:rows]
        other_ref[:, cols] = low(value[rows:])


def branch(sums, got, attended, proj_u, pieces):
    length, columns = attended.shape
    rows, width = length // 2, sum(p.shape[0] for p in pieces)
    ins = (sums, got, attended, proj_u)
    outs = [
        jax.ShapeDtypeStruct((length, columns), narrow),
        jax.ShapeDtypeStruct((length, 1), wide),
        jax.ShapeDtypeStruct((rows, width), wide),
        jax.ShapeDtypeStruct((rows, width), narrow),
    ]
    return pl.pallas_call(
        branch_kernel,
        cost_estimate=cost(2 * length * columns * width, attended, attended, attended, proj_u),
        grid=(1,),
        in_specs=[whole(a) for a in ins] + columns_of(pieces, 1, columns),
        out_specs=[whole(a) for a in outs],
        out_shape=outs,
    )(*ins, *pieces)


def unbranch_kernel(own_ref, other_ref, o_ref, scale_ref, u_ref, *refs):
    pieces, (grad_ref, unit_ref, cross_ref) = refs[:5], refs[5:]
    weight = join(pieces)
    for ref, rows in rows_of((own_ref, other_ref)):
        value = nn(ref[...], weight)
        normed = o_ref[rows, :] * scale_ref[rows, :]
        unit_ref[rows, :] = low(value * normed)
        value = value * u_ref[rows, :]
        grad_ref[rows, :] = value
        cross_ref[:, rows] = row_sums(value * normed)


def unbranch(pair, attended, scale, proj_u, pieces):
    length, columns = attended.shape
    width = pair[0].shape[1]
    ins = (*pair, attended, scale, proj_u)
    outs = [
        jax.ShapeDtypeStruct((length, columns), wide),
        jax.ShapeDtypeStruct((length, columns), narrow),
        jax.ShapeDtypeStruct((8, length), wide),
    ]
    return pl.pallas_call(
        unbranch_kernel,
        cost_estimate=cost(2 * length * columns * width, attended, attended, attended, proj_u),
        grid=(1,),
        in_specs=[whole(a) for a in ins] + columns_of(pieces, 1, columns),
        out_specs=[whole(a) for a in outs],
        out_shape=outs,
    )(*ins, *pieces)


def attend_back_kernel(
    turn_ref,
    rate_ref,
    scale_ref,
    cross_ref,
    got_ref,
    q_ref,
    k_ref,
    v_ref,
    sq_ref,
    sk_ref,
    gn_ref,
    o_ref,
    dq_ref,
    dk_ref,
    dv_ref,
    g_ref,
    c_ref,
    *,
    width,
):
    size = q_ref.shape[0] // 2
    inner, ahead, outof = tables(rate_ref[pl.program_id(0)], size)
    early, late = spans(turn_ref, size)

    @pl.when(pl.program_id(0) == 0)
    def _():
        c_ref[...] = column(cross_ref[...], got_ref[...]) / width

    scale = scale_ref[...]
    normed = o_ref[...] * scale
    g_ref[...] = low(scale * (gn_ref[...] - normed * c_ref[...]))

    def local(rows):
        q, k, v, g = (ref[rows, :] for ref in (q_ref, k_ref, v_ref, g_ref))
        weights = low(nt(q, k) * inner)
        grad_scores = low(nt(g, v) * inner)
        return nn(grad_scores, k), tn(grad_scores, q), tn(weights, g)

    def store(rows, dq, dk, dv):
        dq_ref[rows, :] = low(dq * sq_ref[rows, :].astype(wide))
        dk_ref[rows, :] = low(dk * sk_ref[rows, :].astype(wide))
        dv_ref[rows, :] = low(dv)

    weighted = low(k_ref[early, :].astype(wide) * outof)
    state = low(tn(weighted, v_ref[early, :]))
    g_ahead = low(g_ref[late, :].astype(wide) * ahead)
    grad_state = low(tn(q_ref[late, :], g_ahead))
    dq, dk, dv = local(late)
    store(late, dq + nt(g_ahead, state), dk, dv)
    dq, dk, dv = local(early)
    store(
        early,
        dq,
        dk + nt(v_ref[early, :], grad_state) * outof,
        dv + nn(weighted, grad_state),
    )


def attend_back(turn, rates, scale, cross, got, arrays, width):
    heads = rates.shape[0]
    length, columns = arrays[0].shape
    spec = pl.BlockSpec((length, columns // heads), lambda h: (0, h))
    col = pl.BlockSpec((length, 1), lambda h: (0, 0))
    row = pl.BlockSpec((8, length), lambda h: (0, 0))
    scalar = pl.BlockSpec(memory_space=pltpu.SMEM)
    return pl.pallas_call(
        functools.partial(attend_back_kernel, width=width),
        cost_estimate=cost(12 * length * length * columns, *arrays, *arrays, *arrays),
        grid=(heads,),
        in_specs=[scalar, scalar, col, row, row] + [spec] * len(arrays),
        out_specs=[spec] * 3,
        out_shape=[jax.ShapeDtypeStruct((length, columns), narrow)] * 3,
        scratch_shapes=[
            pltpu.VMEM((length, columns // heads), narrow),
            pltpu.VMEM((length, 1), wide),
        ],
    )(turn, rates, scale, cross, got, *arrays)


def weight_grad_kernel(*refs, count, each):
    pairs, refs = [refs[2 * j : 2 * j + 2] for j in range(each)], refs[2 * each :]
    arrays, outs = refs[:count], refs[count:]
    columns = arrays[0].shape[1]
    for out, cols in cumulative(outs):
        for j, array in enumerate(arrays):
            pair = rows_of(pairs[j % each])
            total = sum(tn(ref[:, cols], array[rows, :]) for ref, rows in pair)
            out[:, j * columns : (j + 1) * columns] = low(total)


def piece_rows(width):
    return [width // 4] * 3 + [width // 8] * 2


def weight_grads(pairs, arrays):
    rows, width = pairs[0][0].shape
    columns = arrays[0].shape[1]
    count = len(arrays)
    return pl.pallas_call(
        functools.partial(weight_grad_kernel, count=count, each=len(pairs)),
        cost_estimate=cost(4 * rows * width * columns * count, *pairs[0], *arrays, *arrays),
        out_shape=[
            jax.ShapeDtypeStruct((r, count * columns), narrow) for r in piece_rows(width)
        ],
    )(*(a for pair in pairs for a in pair), *arrays)


def input_grad_kernel(*refs):
    grads, refs, (own_ref, other_ref) = refs[:4], refs[4:24], refs[24:]
    pieces = [cumulative(refs[5 * j : 5 * j + 5]) for j in range(4)]
    rows = own_ref.shape[0]
    for i in range(5):
        cols = pieces[0][i][1]
        value = sum(nt(grads[j][...], pieces[j][i][0][...]) for j in range(4))
        own_ref[:, cols] = value[:rows]
        other_ref[:, cols] = low(value[rows:])


def input_grad(grads, first, second):
    length, columns = grads[0].shape
    rows, width = length // 2, sum(p.shape[0] for p in first)
    outs = [
        jax.ShapeDtypeStruct((rows, width), wide),
        jax.ShapeDtypeStruct((rows, width), narrow),
    ]
    return pl.pallas_call(
        input_grad_kernel,
        cost_estimate=cost(8 * length * columns * width, *grads, *grads, *grads),
        grid=(1,),
        in_specs=[whole(g) for g in grads]
        + [spec for j in range(3) for spec in columns_of(first, j, columns)]
        + columns_of(second, 0, columns),
        out_specs=[whole(a) for a in outs],
        out_shape=outs,
    )(*grads, *first, *first, *first, *second)


def ffn_kernel(*refs, chained, last):
    n_in, g_in, w_in = refs[0:2], refs[2:4], refs[4:9]
    refs = refs[9:]
    if chained:
        before, refs = refs[:4], refs[4:]
    sums_out, o_out = refs[0:4], refs[4:9]
    n_ref, g_ref, w_ref, s_ref, d_ref, acc_ref, low_ref, o_ref, in_sem, out_sem = refs[9:]
    rows = n_ref.shape[1]
    n = s_ref.shape[2]
    pieces = cumulative(w_in)

    load = [
        pltpu.make_async_copy(ref, w_ref.at[part, :], in_sem.at[4 + i])
        for i, (ref, part) in enumerate(pieces)
    ]
    load += [pltpu.make_async_copy(n_in[h], n_ref.at[h], in_sem.at[h]) for h in range(2)]
    load += [pltpu.make_async_copy(g_in[h], g_ref.at[h], in_sem.at[2 + h]) for h in range(2)]
    for copy in load:
        copy.start()
    accs = [acc_ref.at[k // 2, k % 2] for k in range(4)]
    fill = []
    if chained:
        fill = [pltpu.make_async_copy(before[k], accs[k], in_sem.at[9 + k]) for k in range(4)]
    for copy in fill:
        copy.start()
    for copy in load:
        copy.wait()

    def half(h, carry):
        ab = nn(n_ref[h], w_ref[:, : 2 * n])
        ds = nn(g_ref[h], w_ref[:, 2 * n :])
        a = ab[:, :n]
        b = ab[:, n:]
        s_ref[h] = low(a * b)
        d_ref[h, :, :n] = low(ds * b)
        d_ref[h, :, n:] = low(ds * a)
        return carry

    lax.fori_loop(0, 2, half, 0)
    for copy in fill:
        copy.wait()
    y = nt(s_ref[...].reshape(2 * rows, n), w_ref[:, 2 * n :]).reshape(2, rows, -1)
    d = nt(d_ref[...].reshape(2 * rows, 2 * n), w_ref[:, : 2 * n]).reshape(2, rows, -1)
    for k, value in enumerate((y, d)):
        if chained:
            acc_ref[k] += value
        else:
            acc_ref[k] = value
    stores = []
    for k in range(4):
        source = accs[k]
        if last and k % 2 == 1:
            low_ref[k // 2] = low(acc_ref[k // 2, 1])
            source = low_ref.at[k // 2]
        stores.append(pltpu.make_async_copy(source, sums_out[k], out_sem.at[k]))
        stores[-1].start()
    for i, (_, part) in reversed(list(enumerate(pieces))):
        o_ref[part, : 2 * n] = low(sum(tn(n_ref[h, :, part], d_ref[h]) for h in range(2)))
        o_ref[part, 2 * n :] = low(sum(tn(g_ref[h, :, part], s_ref[h]) for h in range(2)))
        stores.append(pltpu.make_async_copy(o_ref.at[part, :], o_out[i], out_sem.at[4 + i]))
        stores[-1].start()
    for copy in stores:
        copy.wait()


def ffn(normed, grad, pieces, sums, last):
    rows, width = normed[0].shape
    n3 = pieces[0].shape[1]
    n = n3 // 3
    hbm = pl.BlockSpec(memory_space=pl.ANY)
    ins = (*normed, *grad, *pieces, *(sums or ()))
    other = narrow if last else wide
    outs = pl.pallas_call(
        functools.partial(ffn_kernel, chained=sums is not None, last=last),
        cost_estimate=cost(12 * rows * width * n3, *ins, *ins),
        in_specs=[hbm] * len(ins),
        out_specs=[hbm] * 9,
        out_shape=[jax.ShapeDtypeStruct((rows, width), t) for t in (wide, other, wide, other)]
        + [jax.ShapeDtypeStruct((r, n3), narrow) for r in piece_rows(width)],
        scratch_shapes=[
            pltpu.VMEM((2, rows, width), narrow),
            pltpu.VMEM((2, rows, width), narrow),
            pltpu.VMEM((width, n3), narrow),
            pltpu.VMEM((2, rows, n), narrow),
            pltpu.VMEM((2, rows, 2 * n), narrow),
            pltpu.VMEM((2, 2, rows, width), wide),
            pltpu.VMEM((2, rows, width), narrow),
            pltpu.VMEM((width, n3), narrow),
            pltpu.SemaphoreType.DMA((13,)),
            pltpu.SemaphoreType.DMA((9,)),
        ],
    )(*ins)
    return outs[:4], outs[4:]


def ffn_cuts(total):
    cuts = []
    left = total
    while left > 0:
        take = min(tile_width, left)
        cuts.append((total - left, take))
        left -= take
    return cuts


def shards(
    size,
    tokens,
    w_query,
    w_key,
    w_value,
    w_gate,
    w_out,
    w_first,
    w_second,
    w_down,
    decay_rates,
    cotangent,
):
    send = Exchange(size)
    swap = lambda value: lax.ppermute(value, "tensor", [(0, 1), (1, 0)])
    me = lax.axis_index("dp")
    turn = lax.axis_index("tensor").astype(jnp.int32).reshape(1)
    rows, width = tokens.shape
    span = width // size
    offsets = jnp.asarray(np.repeat(block_offsets(size), span))
    place = jnp.bitwise_xor(offsets, me) * span + jnp.arange(width) % span
    shuffle = (jnp.arange(width)[:, None] == place[None, :]).astype(narrow)

    cuts = ffn_cuts(w_first.shape[1])
    down_t = w_down.T
    beside = lambda *arrays: jnp.concatenate(arrays, axis=1)
    first = Gather(send, beside(w_query, w_key, w_value))
    second = Gather(send, beside(w_gate, w_out.T))
    mlp = [
        Gather(send, beside(*(w[:, at : at + n] for w in (w_first, w_second, down_t))))
        for at, n in cuts
    ]
    first.inner(0)
    first.rest()
    second.inner(0, *first.parts[1:])
    first.sides()
    second.rest()
    first.far()
    second.sides(*first.got)
    mlp[0].inner(0, *first.got)

    inputs = low(nn(tokens, shuffle)).astype(wide)
    scale_in = inverse_rms(inputs)
    normed_in = inputs * scale_in
    own_in = low(normed_in)
    pair_in = (own_in, swap(own_in))
    own_cot = low(nn(cotangent, shuffle))
    pair_cot = (own_cot, swap(own_cot))

    pair_in = held_back(pair_in, pair_cot[1])
    query, keys, values, slope_q, slope_k, attended, sums = front(
        turn, decay_rates, pair_in, first.pieces
    )
    attended, sums = held_back((attended, sums), *second.got)
    second.far(attended)
    mlp[0].rest(attended)
    pair_gate = held_back(pair_in, attended)
    mlp[0].sides(*second.last)
    mlp[1].inner(0, attended)
    mlp[1].rest(*second.last)
    mlp[2].inner(0, *second.last)
    proj_u = gate(pair_gate, second.pieces)
    (attended_late,) = held_back((attended,), proj_u)
    gated, scale_out, branch_own, branch_other = branch(
        sums, swap(sums), attended_late, proj_u, second.pieces
    )
    branch_own, branch_other, gated = held_back(
        (branch_own, branch_other, gated), *mlp[0].got, *mlp[1].got, *mlp[2].got
    )
    mlp[0].far(gated)
    mlp[2].rest(gated)
    middle = inputs + branch_own + swap(branch_other).astype(wide)
    scale_mid = inverse_rms(middle)
    normed_mid = middle * scale_mid
    own_mid = low(normed_mid)
    mlp[1].sides(*mlp[0].last)
    mlp[2].sides(*mlp[0].last)
    pair_mid = (own_mid, swap(own_mid))

    pair_mid = held_back(pair_mid, *mlp[2].parts)
    sums, grads = ffn(pair_mid, pair_cot, mlp[0].pieces, None, False)
    outs = [Scatter(send, grads)]
    mlp[1].far(grads[0])
    mlp[2].far(grads[0])
    outs[0].move(grads[0])
    sums, grads = ffn(pair_mid, pair_cot, mlp[1].pieces, sums, False)
    grads = held_back(grads, *mlp[2].last, *outs[0].got)
    outs.append(Scatter(send, grads))
    outs[1].move(grads[0])
    outs[0].move(grads[0])
    pair_mid = held_back(pair_mid, *outs[0].sent)
    sums, grads = ffn(pair_mid, pair_cot, mlp[2].pieces, sums, True)
    outs.append(Scatter(send, grads))
    y_own, y_other, d_own, d_other = held_back(sums, *outs[0].got)
    outs[2].move(d_other)

    grad_mid_norm = d_own + swap(d_other).astype(wide)
    grad_middle = own_cot.astype(wide) + norm_back(grad_mid_norm, normed_mid, scale_mid)
    own_e = low(grad_middle)
    pair_e = (own_e, swap(own_e))
    grad_normed, grad_unit, cross = unbranch(pair_e, attended, scale_out, proj_u, second.pieces)
    other_cross = swap(cross)
    outs[1].move(grad_unit)
    pair_in_late = held_back(pair_in, grad_unit, *outs[1].sent)
    grads = weight_grads((pair_in_late, pair_e), (grad_unit, gated))
    late = Scatter(send, grads)
    outs[0].move(grads[0], other_cross)
    (grad_normed,) = held_back((grad_normed,), grads[0])
    outs[2].move(grads[0])
    grad_q, grad_k, grad_v = held_back(
        attend_back(
            turn,
            decay_rates,
            scale_out,
            cross,
            other_cross,
            (query, keys, values, slope_q, slope_k, grad_normed, attended),
            width,
        ),
        *outs[0].got,
    )
    grads = weight_grads((pair_in,), (grad_q, grad_k, grad_v))
    last = Scatter(send, grads)
    (grad_q_late,) = held_back((grad_q,), grads[0], *outs[1].got, *outs[2].got)
    move_along(outs[1:], grads[0])
    last.move(grads[0])
    late.move(grads[0])
    total_own, total_other = held_back(
        input_grad((grad_q_late, grad_k, grad_v, grad_unit), first.pieces, second.pieces),
        *last.got,
        *late.got,
    )
    last.move(total_own)
    late.move(total_own, *last.sent)
    while len(outs[0].moves) > 1:
        move_along(outs, total_own, *late.sent)
    last.move(*late.sent)
    done = (*last.got, *outs[0].got)
    late.move(*done)
    (y_other,) = held_back((y_other,), *done)
    for out in (*outs, last, late):
        while out.moves:
            out.move(*done)
    grad_in_norm = total_own + swap(total_other).astype(wide)
    tokens_grad = grad_middle + norm_back(grad_in_norm, normed_in, scale_in)
    y_sum = y_own + swap(y_other).astype(wide)
    layer_out = low(middle + y_sum)
    layer_out = low(nt(layer_out, shuffle))
    parts = []
    rest = tokens_grad
    for _ in range(3):
        part = lax.reduce_precision(rest, 8, 7)
        parts.append(low(part))
        rest = rest - part
    tokens_grad = nt(parts[0], shuffle) + (nt(parts[1], shuffle) + nt(parts[2], shuffle))
    thirds = [
        jnp.concatenate(
            [out.total[:, i * n : (i + 1) * n] for out, (_, n) in zip(outs, cuts)], axis=1
        )
        for i in range(3)
    ]
    n = w_query.shape[1]
    return (
        layer_out,
        tokens_grad,
        last.total[:, :n],
        last.total[:, n : 2 * n],
        last.total[:, 2 * n :],
        late.total[:, :n],
        late.total[:, n:].T,
        thirds[0],
        thirds[1],
        thirds[2].T,
    )


def solution(mesh):
    return jax.shard_map(
        functools.partial(shards, mesh.shape["dp"]),
        mesh=mesh,
        in_specs=(
            P(("dp", "tensor"), None),
            P("dp", "tensor"),
            P("dp", "tensor"),
            P("dp", "tensor"),
            P("dp", "tensor"),
            P("tensor", "dp"),
            P("dp", "tensor"),
            P("dp", "tensor"),
            P("tensor", "dp"),
            P("tensor"),
            P(("dp", "tensor"), None),
        ),
        out_specs=(
            P(("dp", "tensor"), None),
            P(("dp", "tensor"), None),
            P("dp", "tensor"),
            P("dp", "tensor"),
            P("dp", "tensor"),
            P("dp", "tensor"),
            P("tensor", "dp"),
            P("dp", "tensor"),
            P("dp", "tensor"),
            P("tensor", "dp"),
        ),
        check_vma=False,
    )
```

```python
import functools

import jax
import jax.numpy as jnp
import numpy as np
from jax import lax
from jax.experimental import pallas as pl
from jax.experimental.pallas import tpu as pltpu
from jax.sharding import PartitionSpec as P

eps = 1e-06
wide = jnp.float32
narrow = jnp.bfloat16
tile_width = 512


def dot(left, right, dims):
    return lax.dot_general(left, right, (dims, ((), ())), preferred_element_type=wide)


def nn(left, right):
    return dot(left, right, ((1,), (0,)))


def nt(left, right):
    return dot(left, right, ((1,), (1,)))


def tn(left, right):
    return dot(left, right, ((0,), (0,)))


def inverse_rms(values):
    return lax.rsqrt(jnp.mean(values * values, axis=-1, keepdims=True) + eps)


def norm_back(grad, normed, scale):
    return scale * (grad - normed * jnp.mean(grad * normed, axis=-1, keepdims=True))


class Exchange:

    def __init__(self, size):
        self.size = size
        self.before = {}

    def __call__(self, array, bit):
        if bit >= 4 and bit in self.before:
            (array,) = held_back((array,), self.before[bit])
        pairs = [(i, i ^ bit) for i in range(self.size)]
        result = lax.ppermute(array, "dp", pairs)
        self.before[bit] = result
        return result


def held_back(values, *waits):
    values = tuple(values)
    if not waits:
        return values
    return lax.optimization_barrier((*values, *waits))[: len(values)]


def inner_bits(size):
    bits = []
    bit = size // 2
    while bit >= 4:
        bits.append(bit)
        bit //= 2
    return bits


def block_offsets(size):
    order = [0]
    for bit in inner_bits(size) + [1, 2]:
        order = order + [entry ^ bit for entry in order]
    return np.array(order, np.int32)


class Gather:

    def __init__(self, send, shard):
        self.send = send
        self.parts = (shard,)

    def join(self, after):
        if after:
            self.parts = held_back(self.parts, *after)
        self.held = jnp.concatenate(self.parts, axis=0)

    def inner(self, level, *after):
        self.join(after)
        bit = inner_bits(self.send.size)[level]
        self.got = (self.send(self.held, bit),)
        self.parts = (self.held, *self.got)

    def rest(self, *after):
        for level in range(1, len(inner_bits(self.send.size))):
            self.inner(level, *after)

    def sides(self, *after):
        self.join(after)
        self.got = (self.send(self.held, 1), self.send(self.held, 2))

    def far(self, *after):
        half = self.held.shape[0] // 2
        side, up = held_back(self.got, *after)
        self.last = (self.send(side[:half], 2), self.send(up[half:], 1))
        self.pieces = [self.held, *self.got, *self.last]


def low(value):
    return value.astype(narrow)


def merge_kernel(up_ref, side_ref, to_up_ref, to_side_ref, up_out, side_out):
    up_out[...] = low(up_ref[...].astype(wide) + to_up_ref[...].astype(wide))
    side_out[...] = low(side_ref[...].astype(wide) + to_side_ref[...].astype(wide))


def merge(up, side, to_up, to_side):
    half = to_up.shape
    block = lambda i: pl.BlockSpec(half, lambda _: (i, 0))
    return pl.pallas_call(
        merge_kernel,
        grid=(1,),
        in_specs=[block(0), block(1), block(0), block(0)],
        out_specs=[block(0), block(1)],
        out_shape=[jax.ShapeDtypeStruct(a.shape, a.dtype) for a in (up, side)],
        input_output_aliases={0: 0, 1: 1},
        cost_estimate=cost(up.size, up, up, up),
    )(up, side, to_up, to_side)


class Scatter:

    def __init__(self, send, pieces):
        self.send = send
        self.first, self.side, self.up, *self.away = pieces
        self.moves = ["far", "sides", *reversed(inner_bits(send.size)), "end"]
        self.rest = None

    def move(self, *after):
        name = self.moves.pop(0)
        if name == "far":
            away = held_back(self.away, *after)
            self.got = tuple(self.send(a, b) for a, b in zip(away, (1, 2)))
            return
        if name == "sides":
            self.got = held_back(self.got, *after)
            self.sent = merge(self.up, self.side, *self.got)
            self.got = (self.send(self.sent[1], 1), self.send(self.sent[0], 2))
        elif name == "end":
            self.add(after)
        else:
            self.add(after)
            self.got = (self.send(self.split(), name),)

    def add(self, after):
        got = held_back(self.got, *after)
        rest = self.first.astype(wide) if self.rest is None else self.rest
        self.total = rest + sum(g.astype(wide) for g in got)

    def split(self):
        half = self.total.shape[0] // 2
        self.rest = self.total[:half]
        return low(self.total[half:])


def move_along(scatters, *after):
    name = scatters[0].moves[0]
    assert all(out.moves[0] == name for out in scatters)
    parts = []
    for out in scatters:
        out.moves.pop(0)
        out.add(after)
        parts.append(out.split())
    got = scatters[0].send(jnp.concatenate(parts, axis=1), name)
    at = 0
    for out, part in zip(scatters, parts):
        out.got = (got[:, at : at + part.shape[1]],)
        at += part.shape[1]


def tables(rate, size):
    row = lax.broadcasted_iota(jnp.int32, (size, 1), 0).astype(wide)
    col = lax.broadcasted_iota(jnp.int32, (1, size), 1).astype(wide)
    ahead = jnp.exp(-rate * row)
    inner = jnp.where(col <= row, ahead * jnp.exp(rate * col), 0.0)
    outof = jnp.exp(-rate * (size - row))
    return inner, ahead, outof


def cost(flops, *arrays):
    size = sum(a.size * jnp.dtype(a.dtype).itemsize for a in arrays)
    return pl.CostEstimate(flops=int(flops), transcendentals=0, bytes_accessed=int(size))


def rows_of(refs):
    half = refs[0].shape[0]
    return [(ref, slice(i * half, (i + 1) * half)) for i, ref in enumerate(refs)]


def join(refs):
    return jnp.concatenate([ref[...] for ref in refs], axis=0)


def row_sums(values):
    ones = jnp.ones((8, values.shape[1]), wide)
    return lax.dot_general(
        ones,
        values,
        (((1,), (1,)), ((), ())),
        precision=lax.Precision.HIGHEST,
        preferred_element_type=wide,
    )


def column(own, other):
    half = own.shape[1] // 2
    total = own + jnp.concatenate([other[:, half:], other[:, :half]], axis=1)
    return jnp.transpose(total)[:, :1]


def spans(turn_ref, size):
    turn = turn_ref[0]
    early = pl.ds(pl.multiple_of(turn * size, size), size)
    late = pl.ds(pl.multiple_of((1 - turn) * size, size), size)
    return early, late


def cumulative(refs):
    at = 0
    result = []
    for ref in refs:
        result.append((ref, slice(at, at + ref.shape[0])))
        at += ref.shape[0]
    return result


def whole(array):
    return pl.BlockSpec(array.shape, lambda i: (0, 0))


def columns_of(pieces, j, width):
    return [pl.BlockSpec((p.shape[0], width), lambda i: (0, j)) for p in pieces]


def front_kernel(turn_ref, rate_ref, own_ref, other_ref, *refs, heads):
    wq, wk, wv = refs[0:5], refs[5:10], refs[10:15]
    q_ref, k_ref, v_ref, sq_ref, sk_ref, o_ref, sum_ref = refs[15:]
    pair = rows_of((own_ref, other_ref))
    for pieces, out, slope in ((wq, q_ref, sq_ref), (wk, k_ref, sk_ref)):
        weight = join(pieces)
        for ref, rows in pair:
            value = nn(ref[...], weight)
            sigma = jax.nn.sigmoid(value)
            out[rows, :] = low(value * sigma)
            slope[rows, :] = low(sigma * (1.0 + value * (1.0 - sigma)))
    weight = join(wv)
    for ref, rows in pair:
        v_ref[rows, :] = low(nn(ref[...], weight))
    size = own_ref.shape[0]
    early, late = spans(turn_ref, size)
    wide_head = q_ref.shape[1] // heads
    sums = 0.0
    for j in range(heads):
        cols = slice(j * wide_head, (j + 1) * wide_head)
        inner, ahead, outof = tables(rate_ref[pl.program_id(0) * heads + j], size)

        def local(rows):
            weights = low(nt(q_ref[rows, cols], k_ref[rows, cols]) * inner)
            return nn(weights, v_ref[rows, cols])

        weighted = low(k_ref[early, cols].astype(wide) * outof)
        state = low(tn(weighted, v_ref[early, cols]))
        o_ref[early, cols] = local(early)
        o_ref[late, cols] = local(late) + nn(q_ref[late, cols], state) * ahead
    values = o_ref[...]
    sums = row_sums(values * values)

    @pl.when(pl.program_id(0) == 0)
    def _():
        sum_ref[...] = sums

    @pl.when(pl.program_id(0) > 0)
    def _():
        sum_ref[...] += sums


def front(turn, rates, pair, pieces):
    rows, width = pair[0].shape
    columns = pieces[0].shape[1] // 3
    steps = 2
    block = columns // steps
    scalar = pl.BlockSpec(memory_space=pltpu.SMEM)
    piece = lambda p, j: pl.BlockSpec((p.shape[0], block), lambda i: (0, i + steps * j))
    out = pl.BlockSpec((2 * rows, block), lambda i: (0, i))
    sums = jax.ShapeDtypeStruct((8, 2 * rows), wide)
    types = [narrow] * 5 + [wide]
    return pl.pallas_call(
        functools.partial(front_kernel, heads=rates.shape[0] // steps),
        cost_estimate=cost(18 * rows * width * columns, *pair, *pair, *pair, *pair, *pair),
        grid=(steps,),
        in_specs=[scalar, scalar]
        + [whole(p) for p in pair]
        + [piece(p, j) for j in range(3) for p in pieces],
        out_specs=[out] * 6 + [whole(sums)],
        out_shape=[jax.ShapeDtypeStruct((2 * rows, columns), t) for t in types] + [sums],
    )(turn, rates, *pair, *pieces, *pieces, *pieces)


def gate_kernel(own_ref, other_ref, *refs):
    weight = join(refs[:-1])
    for ref, rows in rows_of((own_ref, other_ref)):
        refs[-1][rows, :] = nn(ref[...], weight).astype(refs[-1].dtype)


def gate(pair, pieces):
    rows, width = pair[0].shape
    columns = pieces[0].shape[1] // 2
    out = jax.ShapeDtypeStruct((2 * rows, columns), wide)
    return pl.pallas_call(
        gate_kernel,
        cost_estimate=cost(4 * rows * width * columns, *pair, *pair),
        grid=(1,),
        in_specs=[whole(p) for p in pair] + columns_of(pieces, 0, columns),
        out_specs=whole(out),
        out_shape=out,
    )(*pair, *pieces)


def branch_kernel(sum_ref, got_ref, o_ref, u_ref, *refs):
    pieces, (gated_ref, scale_ref, own_ref, other_ref) = refs[:5], refs[5:]
    rows, width = own_ref.shape
    scale = lax.rsqrt(column(sum_ref[...], got_ref[...]) / width + eps)
    scale_ref[...] = scale
    gated_ref[...] = low(o_ref[...] * scale * u_ref[...])
    for ref, cols in cumulative(pieces):
        value = nt(gated_ref[...], ref[...])
        own_ref[:, cols] = value[:rows]
        other_ref[:, cols] = low(value[rows:])


def branch(sums, got, attended, proj_u, pieces):
    length, columns = attended.shape
    rows, width = length // 2, sum(p.shape[0] for p in pieces)
    ins = (sums, got, attended, proj_u)
    outs = [
        jax.ShapeDtypeStruct((length, columns), narrow),
        jax.ShapeDtypeStruct((length, 1), wide),
        jax.ShapeDtypeStruct((rows, width), wide),
        jax.ShapeDtypeStruct((rows, width), narrow),
    ]
    return pl.pallas_call(
        branch_kernel,
        cost_estimate=cost(2 * length * columns * width, attended, attended, attended, proj_u),
        grid=(1,),
        in_specs=[whole(a) for a in ins] + columns_of(pieces, 1, columns),
        out_specs=[whole(a) for a in outs],
        out_shape=outs,
    )(*ins, *pieces)


def unbranch_kernel(own_ref, other_ref, o_ref, scale_ref, u_ref, *refs):
    pieces, (grad_ref, unit_ref, cross_ref) = refs[:5], refs[5:]
    weight = join(pieces)
    for ref, rows in rows_of((own_ref, other_ref)):
        value = nn(ref[...], weight)
        normed = o_ref[rows, :] * scale_ref[rows, :]
        unit_ref[rows, :] = low(value * normed)
        value = value * u_ref[rows, :]
        grad_ref[rows, :] = value
        cross_ref[:, rows] = row_sums(value * normed)


def unbranch(pair, attended, scale, proj_u, pieces):
    length, columns = attended.shape
    width = pair[0].shape[1]
    ins = (*pair, attended, scale, proj_u)
    outs = [
        jax.ShapeDtypeStruct((length, columns), wide),
        jax.ShapeDtypeStruct((length, columns), narrow),
        jax.ShapeDtypeStruct((8, length), wide),
    ]
    return pl.pallas_call(
        unbranch_kernel,
        cost_estimate=cost(2 * length * columns * width, attended, attended, attended, proj_u),
        grid=(1,),
        in_specs=[whole(a) for a in ins] + columns_of(pieces, 1, columns),
        out_specs=[whole(a) for a in outs],
        out_shape=outs,
    )(*ins, *pieces)


def attend_back_kernel(
    turn_ref,
    rate_ref,
    scale_ref,
    cross_ref,
    got_ref,
    q_ref,
    k_ref,
    v_ref,
    sq_ref,
    sk_ref,
    gn_ref,
    o_ref,
    dq_ref,
    dk_ref,
    dv_ref,
    g_ref,
    c_ref,
    *,
    width,
):
    size = q_ref.shape[0] // 2
    inner, ahead, outof = tables(rate_ref[pl.program_id(0)], size)
    early, late = spans(turn_ref, size)

    @pl.when(pl.program_id(0) == 0)
    def _():
        c_ref[...] = column(cross_ref[...], got_ref[...]) / width

    scale = scale_ref[...]
    normed = o_ref[...] * scale
    g_ref[...] = low(scale * (gn_ref[...] - normed * c_ref[...]))

    def local(rows):
        q, k, v, g = (ref[rows, :] for ref in (q_ref, k_ref, v_ref, g_ref))
        weights = low(nt(q, k) * inner)
        grad_scores = low(nt(g, v) * inner)
        return nn(grad_scores, k), tn(grad_scores, q), tn(weights, g)

    def store(rows, dq, dk, dv):
        dq_ref[rows, :] = low(dq * sq_ref[rows, :].astype(wide))
        dk_ref[rows, :] = low(dk * sk_ref[rows, :].astype(wide))
        dv_ref[rows, :] = low(dv)

    weighted = low(k_ref[early, :].astype(wide) * outof)
    state = low(tn(weighted, v_ref[early, :]))
    g_ahead = low(g_ref[late, :].astype(wide) * ahead)
    grad_state = low(tn(q_ref[late, :], g_ahead))
    dq, dk, dv = local(late)
    store(late, dq + nt(g_ahead, state), dk, dv)
    dq, dk, dv = local(early)
    store(
        early,
        dq,
        dk + nt(v_ref[early, :], grad_state) * outof,
        dv + nn(weighted, grad_state),
    )


def attend_back(turn, rates, scale, cross, got, arrays, width):
    heads = rates.shape[0]
    length, columns = arrays[0].shape
    spec = pl.BlockSpec((length, columns // heads), lambda h: (0, h))
    col = pl.BlockSpec((length, 1), lambda h: (0, 0))
    row = pl.BlockSpec((8, length), lambda h: (0, 0))
    scalar = pl.BlockSpec(memory_space=pltpu.SMEM)
    return pl.pallas_call(
        functools.partial(attend_back_kernel, width=width),
        cost_estimate=cost(12 * length * length * columns, *arrays, *arrays, *arrays),
        grid=(heads,),
        in_specs=[scalar, scalar, col, row, row] + [spec] * len(arrays),
        out_specs=[spec] * 3,
        out_shape=[jax.ShapeDtypeStruct((length, columns), narrow)] * 3,
        scratch_shapes=[
            pltpu.VMEM((length, columns // heads), narrow),
            pltpu.VMEM((length, 1), wide),
        ],
    )(turn, rates, scale, cross, got, *arrays)


def weight_grad_kernel(*refs, count, each):
    pairs, refs = [refs[2 * j : 2 * j + 2] for j in range(each)], refs[2 * each :]
    arrays, outs = refs[:count], refs[count:]
    columns = arrays[0].shape[1]
    for out, cols in cumulative(outs):
        for j, array in enumerate(arrays):
            pair = rows_of(pairs[j % each])
            total = sum(tn(ref[:, cols], array[rows, :]) for ref, rows in pair)
            out[:, j * columns : (j + 1) * columns] = low(total)


def piece_rows(width):
    return [width // 4] * 3 + [width // 8] * 2


def weight_grads(pairs, arrays):
    rows, width = pairs[0][0].shape
    columns = arrays[0].shape[1]
    count = len(arrays)
    return pl.pallas_call(
        functools.partial(weight_grad_kernel, count=count, each=len(pairs)),
        cost_estimate=cost(4 * rows * width * columns * count, *pairs[0], *arrays, *arrays),
        out_shape=[
            jax.ShapeDtypeStruct((r, count * columns), narrow) for r in piece_rows(width)
        ],
    )(*(a for pair in pairs for a in pair), *arrays)


def input_grad_kernel(*refs):
    grads, refs, (own_ref, other_ref) = refs[:4], refs[4:24], refs[24:]
    pieces = [cumulative(refs[5 * j : 5 * j + 5]) for j in range(4)]
    rows = own_ref.shape[0]
    for i in range(5):
        cols = pieces[0][i][1]
        value = sum(nt(grads[j][...], pieces[j][i][0][...]) for j in range(4))
        own_ref[:, cols] = value[:rows]
        other_ref[:, cols] = low(value[rows:])


def input_grad(grads, first, second):
    length, columns = grads[0].shape
    rows, width = length // 2, sum(p.shape[0] for p in first)
    outs = [
        jax.ShapeDtypeStruct((rows, width), wide),
        jax.ShapeDtypeStruct((rows, width), narrow),
    ]
    return pl.pallas_call(
        input_grad_kernel,
        cost_estimate=cost(8 * length * columns * width, *grads, *grads, *grads),
        grid=(1,),
        in_specs=[whole(g) for g in grads]
        + [spec for j in range(3) for spec in columns_of(first, j, columns)]
        + columns_of(second, 0, columns),
        out_specs=[whole(a) for a in outs],
        out_shape=outs,
    )(*grads, *first, *first, *first, *second)


def ffn_kernel(*refs, chained, last):
    n_in, g_in, w_in = refs[0:2], refs[2:4], refs[4:9]
    refs = refs[9:]
    if chained:
        before, refs = refs[:4], refs[4:]
    sums_out, o_out = refs[0:4], refs[4:9]
    n_ref, g_ref, w_ref, s_ref, d_ref, acc_ref, low_ref, o_ref, in_sem, out_sem = refs[9:]
    rows = n_ref.shape[1]
    n = s_ref.shape[2]
    pieces = cumulative(w_in)

    load = [
        pltpu.make_async_copy(ref, w_ref.at[part, :], in_sem.at[4 + i])
        for i, (ref, part) in enumerate(pieces)
    ]
    load += [pltpu.make_async_copy(n_in[h], n_ref.at[h], in_sem.at[h]) for h in range(2)]
    load += [pltpu.make_async_copy(g_in[h], g_ref.at[h], in_sem.at[2 + h]) for h in range(2)]
    for copy in load:
        copy.start()
    accs = [acc_ref.at[k // 2, k % 2] for k in range(4)]
    fill = []
    if chained:
        fill = [pltpu.make_async_copy(before[k], accs[k], in_sem.at[9 + k]) for k in range(4)]
    for copy in fill:
        copy.start()
    for copy in load:
        copy.wait()

    def half(h, carry):
        ab = nn(n_ref[h], w_ref[:, : 2 * n])
        ds = nn(g_ref[h], w_ref[:, 2 * n :])
        a = ab[:, :n]
        b = ab[:, n:]
        s_ref[h] = low(a * b)
        d_ref[h, :, :n] = low(ds * b)
        d_ref[h, :, n:] = low(ds * a)
        return carry

    lax.fori_loop(0, 2, half, 0)
    for copy in fill:
        copy.wait()
    y = nt(s_ref[...].reshape(2 * rows, n), w_ref[:, 2 * n :]).reshape(2, rows, -1)
    d = nt(d_ref[...].reshape(2 * rows, 2 * n), w_ref[:, : 2 * n]).reshape(2, rows, -1)
    for k, value in enumerate((y, d)):
        if chained:
            acc_ref[k] += value
        else:
            acc_ref[k] = value
    stores = []
    for k in range(4):
        source = accs[k]
        if last and k % 2 == 1:
            low_ref[k // 2] = low(acc_ref[k // 2, 1])
            source = low_ref.at[k // 2]
        stores.append(pltpu.make_async_copy(source, sums_out[k], out_sem.at[k]))
        stores[-1].start()
    for i, (_, part) in reversed(list(enumerate(pieces))):
        o_ref[part, : 2 * n] = low(sum(tn(n_ref[h, :, part], d_ref[h]) for h in range(2)))
        o_ref[part, 2 * n :] = low(sum(tn(g_ref[h, :, part], s_ref[h]) for h in range(2)))
        stores.append(pltpu.make_async_copy(o_ref.at[part, :], o_out[i], out_sem.at[4 + i]))
        stores[-1].start()
    for copy in stores:
        copy.wait()


def ffn(normed, grad, pieces, sums, last):
    rows, width = normed[0].shape
    n3 = pieces[0].shape[1]
    n = n3 // 3
    hbm = pl.BlockSpec(memory_space=pl.ANY)
    ins = (*normed, *grad, *pieces, *(sums or ()))
    other = narrow if last else wide
    outs = pl.pallas_call(
        functools.partial(ffn_kernel, chained=sums is not None, last=last),
        cost_estimate=cost(12 * rows * width * n3, *ins, *ins),
        in_specs=[hbm] * len(ins),
        out_specs=[hbm] * 9,
        out_shape=[jax.ShapeDtypeStruct((rows, width), t) for t in (wide, other, wide, other)]
        + [jax.ShapeDtypeStruct((r, n3), narrow) for r in piece_rows(width)],
        scratch_shapes=[
            pltpu.VMEM((2, rows, width), narrow),
            pltpu.VMEM((2, rows, width), narrow),
            pltpu.VMEM((width, n3), narrow),
            pltpu.VMEM((2, rows, n), narrow),
            pltpu.VMEM((2, rows, 2 * n), narrow),
            pltpu.VMEM((2, 2, rows, width), wide),
            pltpu.VMEM((2, rows, width), narrow),
            pltpu.VMEM((width, n3), narrow),
            pltpu.SemaphoreType.DMA((13,)),
            pltpu.SemaphoreType.DMA((9,)),
        ],
    )(*ins)
    return outs[:4], outs[4:]


def ffn_cuts(total):
    cuts = []
    left = total
    while left > 0:
        take = min(tile_width, left)
        cuts.append((total - left, take))
        left -= take
    return cuts


def shards(
    size,
    tokens,
    w_query,
    w_key,
    w_value,
    w_gate,
    w_out,
    w_first,
    w_second,
    w_down,
    decay_rates,
    cotangent,
):
    send = Exchange(size)
    swap = lambda value: lax.ppermute(value, "tensor", [(0, 1), (1, 0)])
    me = lax.axis_index("dp")
    turn = lax.axis_index("tensor").astype(jnp.int32).reshape(1)
    rows, width = tokens.shape
    span = width // size
    offsets = jnp.asarray(np.repeat(block_offsets(size), span))
    place = jnp.bitwise_xor(offsets, me) * span + jnp.arange(width) % span
    shuffle = (jnp.arange(width)[:, None] == place[None, :]).astype(narrow)

    cuts = ffn_cuts(w_first.shape[1])
    down_t = w_down.T
    beside = lambda *arrays: jnp.concatenate(arrays, axis=1)
    first = Gather(send, beside(w_query, w_key, w_value))
    second = Gather(send, beside(w_gate, w_out.T))
    mlp = [
        Gather(send, beside(*(w[:, at : at + n] for w in (w_first, w_second, down_t))))
        for at, n in cuts
    ]
    first.inner(0)
    first.rest()
    second.inner(0, *first.parts[1:])
    first.sides()
    second.rest()
    first.far()
    second.sides(*first.got)
    mlp[0].inner(0, *first.got)

    inputs = low(nn(tokens, shuffle)).astype(wide)
    scale_in = inverse_rms(inputs)
    normed_in = inputs * scale_in
    own_in = low(normed_in)
    pair_in = (own_in, swap(own_in))
    own_cot = low(nn(cotangent, shuffle))
    pair_cot = (own_cot, swap(own_cot))

    pair_in = held_back(pair_in, pair_cot[1])
    query, keys, values, slope_q, slope_k, attended, sums = front(
        turn, decay_rates, pair_in, first.pieces
    )
    attended, sums = held_back((attended, sums), *second.got)
    second.far(attended)
    mlp[0].rest(attended)
    pair_gate = held_back(pair_in, attended)
    mlp[0].sides(*second.last)
    mlp[1].inner(0, attended)
    mlp[1].rest(*second.last)
    mlp[2].inner(0, *second.last)
    proj_u = gate(pair_gate, second.pieces)
    (attended_late,) = held_back((attended,), proj_u)
    gated, scale_out, branch_own, branch_other = branch(
        sums, swap(sums), attended_late, proj_u, second.pieces
    )
    branch_own, branch_other, gated = held_back(
        (branch_own, branch_other, gated), *mlp[0].got, *mlp[1].got, *mlp[2].got
    )
    mlp[0].far(gated)
    mlp[2].rest(gated)
    middle = inputs + branch_own + swap(branch_other).astype(wide)
    scale_mid = inverse_rms(middle)
    normed_mid = middle * scale_mid
    own_mid = low(normed_mid)
    mlp[1].sides(*mlp[0].last)
    mlp[2].sides(*mlp[0].last)
    pair_mid = (own_mid, swap(own_mid))

    pair_mid = held_back(pair_mid, *mlp[2].parts)
    sums, grads = ffn(pair_mid, pair_cot, mlp[0].pieces, None, False)
    outs = [Scatter(send, grads)]
    mlp[1].far(grads[0])
    mlp[2].far(grads[0])
    outs[0].move(grads[0])
    sums, grads = ffn(pair_mid, pair_cot, mlp[1].pieces, sums, False)
    grads = held_back(grads, *mlp[2].last, *outs[0].got)
    outs.append(Scatter(send, grads))
    outs[1].move(grads[0])
    outs[0].move(grads[0])
    pair_mid = held_back(pair_mid, *outs[0].sent)
    sums, grads = ffn(pair_mid, pair_cot, mlp[2].pieces, sums, True)
    outs.append(Scatter(send, grads))
    y_own, y_other, d_own, d_other = held_back(sums, *outs[0].got)
    outs[2].move(d_other)

    grad_mid_norm = d_own + swap(d_other).astype(wide)
    grad_middle = own_cot.astype(wide) + norm_back(grad_mid_norm, normed_mid, scale_mid)
    own_e = low(grad_middle)
    pair_e = (own_e, swap(own_e))
    grad_normed, grad_unit, cross = unbranch(pair_e, attended, scale_out, proj_u, second.pieces)
    other_cross = swap(cross)
    outs[1].move(grad_unit)
    pair_in_late = held_back(pair_in, grad_unit, *outs[1].sent)
    grads = weight_grads((pair_in_late, pair_e), (grad_unit, gated))
    late = Scatter(send, grads)
    outs[0].move(grads[0], other_cross)
    (grad_normed,) = held_back((grad_normed,), grads[0])
    outs[2].move(grads[0])
    grad_q, grad_k, grad_v = held_back(
        attend_back(
            turn,
            decay_rates,
            scale_out,
            cross,
            other_cross,
            (query, keys, values, slope_q, slope_k, grad_normed, attended),
            width,
        ),
        *outs[0].got,
    )
    grads = weight_grads((pair_in,), (grad_q, grad_k, grad_v))
    last = Scatter(send, grads)
    (grad_q_late,) = held_back((grad_q,), grads[0], *outs[1].got, *outs[2].got)
    move_along(outs[1:], grads[0])
    last.move(grads[0])
    late.move(grads[0])
    total_own, total_other = held_back(
        input_grad((grad_q_late, grad_k, grad_v, grad_unit), first.pieces, second.pieces),
        *last.got,
        *late.got,
    )
    last.move(total_own)
    late.move(total_own, *last.sent)
    while len(outs[0].moves) > 1:
        move_along(outs, total_own, *late.sent)
    (total_other,) = held_back((total_other,), *last.got)
    last.move(*late.sent)
    done = (*last.got, *outs[0].got)
    late.move(*done)
    (y_other,) = held_back((y_other,), *done)
    for out in (*outs, last, late):
        while len(out.moves) > 1:
            out.move(*done)
    for out in (*outs, last):
        out.move(*done)
    grad_in_norm = total_own + swap(total_other).astype(wide)
    tokens_grad = grad_middle + norm_back(grad_in_norm, normed_in, scale_in)
    y_sum = y_own + swap(y_other).astype(wide)
    layer_out = low(middle + y_sum)
    layer_out = low(nt(layer_out, shuffle))
    late.move(layer_out)
    parts = []
    rest = tokens_grad
    for _ in range(3):
        part = lax.reduce_precision(rest, 8, 7)
        parts.append(low(part))
        rest = rest - part
    tokens_grad = nt(parts[0], shuffle) + (nt(parts[1], shuffle) + nt(parts[2], shuffle))
    thirds = [
        jnp.concatenate(
            [out.total[:, i * n : (i + 1) * n] for out, (_, n) in zip(outs, cuts)], axis=1
        )
        for i in range(3)
    ]
    n = w_query.shape[1]
    return (
        layer_out,
        tokens_grad,
        last.total[:, :n],
        last.total[:, n : 2 * n],
        last.total[:, 2 * n :],
        late.total[:, :n],
        late.total[:, n:].T,
        thirds[0],
        thirds[1],
        thirds[2].T,
    )


def solution(mesh):
    return jax.shard_map(
        functools.partial(shards, mesh.shape["dp"]),
        mesh=mesh,
        in_specs=(
            P(("dp", "tensor"), None),
            P("dp", "tensor"),
            P("dp", "tensor"),
            P("dp", "tensor"),
            P("dp", "tensor"),
            P("tensor", "dp"),
            P("dp", "tensor"),
            P("dp", "tensor"),
            P("tensor", "dp"),
            P("tensor"),
            P(("dp", "tensor"), None),
        ),
        out_specs=(
            P(("dp", "tensor"), None),
            P(("dp", "tensor"), None),
            P("dp", "tensor"),
            P("dp", "tensor"),
            P("dp", "tensor"),
            P("dp", "tensor"),
            P("tensor", "dp"),
            P("dp", "tensor"),
            P("dp", "tensor"),
            P("tensor", "dp"),
        ),
        check_vma=False,
    )
```
